256 devices in a mesh: blk: 64 (over y, z, core), sp: 4 (over x).
Axes of the slice: x: 4, y: 4, z: 8, core: 2. Of those that a mesh axis runs over, the one named last changes fastest.
Arguments:
- species: float32 [8, 2048, 4096], P('sp', 'blk'), may hold values from 0 to 0.25
- interface_normal_flow: float32 [3, 2048, 4096], P(None, 'blk'), may hold values from -6 to 6
- face_diffusion: float32 [3, 2048, 4096], P(None, 'blk'), may hold values from 0.3 to 3
- inv_volume: float32 [2048, 4096], P('blk'), may hold values from 0.5 to 2
- diffusivity: float32 [8], P('sp'), may hold values from 0.2 to 2
- low_partner: int32 [64, 64], P('blk'), may hold values from 0 to 63, as said below
- high_partner: int32 [64, 64], P('blk'), may hold values from 0 to 63, as said below
- low_orient: int32 [64, 64], P('blk'), may hold values from 0 to 7
- high_orient: int32 [64, 64], P('blk'), may hold values from 0 to 7, as said below
- droplet_table: float32 [65536, 128], P(('blk', 'sp')), may hold values from -6 to 6
- parcel_block: int32 [65536, 1], P(('blk', 'sp')), may hold values from 0 to 63; in each aligned block of 256 rows (0 to 255, 256 to 511, ...) at most 6 rows name the same one
- parcel_cell: int32 [65536], P(('blk', 'sp')), may hold values from 0 to 131071
- parcel_live: int32 [65536], P(('blk', 'sp')), may hold values 0 or 1
Outputs:
- new_species: float32 [8, 2048, 4096], P('sp', 'blk')
- arrived: float32 [98304, 128], P(('blk', 'sp'))
The draws below stay inside these ranges and needn't reach their ends.
Inputs may be any that keep to these rules, and one draw needn't show every extreme that they name: low_partner: in each row no block appears more than 1 times and some block appears exactly 1 times; high_partner[c, t] = b exactly when low_partner[b, t] = c. high_partner: in each row no block appears more than 1 times and some block appears exactly 1 times. high_orient[c, t] = low_orient[high_partner[c, t], t]. parcel_block: among the slots of one device no block is named more than 6 times.
All inputs are finite; a program needn't handle non-finite values. No bound on the sum of `parcel_live` on one device may be relied on, other than what follows from the above.
Results may differ from the reference program's by a relative error of at most 0.00002.
Values sent between devices are 32-bit elements; how exact they have to be, the bound alone decides.
A program may use at most 192 MiB of HBM per device.

```python
import math
import jax
import jax.numpy as jnp
import numpy as np
from jax import lax

NSPEC = 8
PV = 128
BJ = 64
BK = 64
TILE_SIDE = 8
CI = 32
PAR_DEV = 256
NBLOCKS = 64
JK = 4096
TILES = 64
PCAP = 6
N_SP = 4


def matching(key):
    base_key = jax.random.fold_in(key, 4711)
    key_outer, key_inner, key_shift, key_orient = jax.random.split(base_key, 4)
    outer_order = jax.random.permutation(key_outer, NBLOCKS).astype(jnp.int32)
    inner_order = jax.random.permutation(key_inner, NBLOCKS).astype(jnp.int32)
    shifts = jax.random.permutation(key_shift, NBLOCKS).astype(jnp.int32)[jnp.arange(TILES) % NBLOCKS]
    numbers = jnp.arange(NBLOCKS, dtype=jnp.int32)
    outer_inverse = jnp.zeros((NBLOCKS,), jnp.int32).at[outer_order].set(numbers)
    inner_inverse = jnp.zeros((NBLOCKS,), jnp.int32).at[inner_order].set(numbers)
    low_partner = outer_order[(inner_order[:, None] + shifts[None, :]) % NBLOCKS]
    high_partner = inner_inverse[(outer_inverse[:, None] - shifts[None, :]) % NBLOCKS]
    low_orient = jax.random.randint(key_orient, (NBLOCKS, TILES), 0, 8).astype(jnp.int32)
    high_orient = low_orient[high_partner, jnp.arange(TILES)[None, :]]
    return (low_partner.astype(jnp.int32), high_partner.astype(jnp.int32), low_orient, high_orient.astype(jnp.int32))


def draw_low_partner(key, part):
    return matching(key)[0]


def draw_high_partner(key, part):
    return matching(key)[1]


def draw_low_orient(key, part):
    return matching(key)[2]


def draw_high_orient(key, part):
    return matching(key)[3]


def set_ends(array, own_key, least, largest):
    index_at = [jax.random.randint(jax.random.fold_in(own_key, axis), (), 0, length) for axis, length in enumerate(array.shape)]
    widest = array.shape.index(max(array.shape))
    next_to = index_at[:widest] + [(index_at[widest] + 1) % array.shape[widest]] + index_at[widest + 1:]
    return array.at[tuple(index_at)].set(least).at[tuple(next_to)].set(largest)


def block_levels(rng, dims, shards, smallest, top_value):
    def one(axis_at, parts):
        heights = jax.random.uniform(jax.random.fold_in(jax.random.fold_in(rng, 6), axis_at), (parts,), jnp.float32, smallest / len(shards), top_value / len(shards))
        return jnp.repeat(jnp.exp(heights), dims[axis_at] // parts).reshape((-1,) + (1,) * (len(dims) - axis_at - 1))

    loudness = one(*shards[0])
    for cut in shards[1:]:
        loudness = loudness * one(*cut)
    return loudness


def assign_block(stream_key, own, number, rows, count, top, limit, lean):
    sequence = jax.random.permutation(stream_key, count)
    packed, usual = load_shares(count, rows * top, limit, lean, True), load_shares(count, rows * top, limit, lean, False)
    places = jnp.arange(count)

    def named(tallies, turn):
        used = int((tallies > 0).sum())
        fixed = max(1, used // 4)
        shifted = fixed + (places - fixed + turn * (used - fixed)) % max(1, count - fixed)
        return jnp.zeros((count,), jnp.int32).at[sequence[jnp.where(places < fixed, places, shifted)]].set(jnp.asarray(tallies, jnp.int32))

    tallies = jnp.where(number % 4 == 0, named(packed, number // 4), named(usual, number - number // 4 - 1))
    mixed = jax.random.permutation(jax.random.fold_in(own, 3), count)
    giver, taker = mixed[0:count // 2 * 2:2], mixed[1:count // 2 * 2:2]
    slack = jnp.minimum(tallies[giver] - 1, limit - tallies[taker]) // 2
    slack = jnp.where((giver == sequence[0]) | (taker == sequence[0]) | (tallies[taker] == 0), 0, jnp.maximum(slack, 0))
    shifted = jax.random.randint(jax.random.fold_in(own, 4), (count // 2,), 0, 1 << 20) % (slack + 1)
    tallies = tallies.at[giver].add(-shifted).at[taker].add(shifted)
    members = jnp.searchsorted(jnp.cumsum(tallies), jnp.arange(rows * top), side="right").astype(jnp.int32)
    table = members.reshape(top, rows).T
    table = table[jax.random.permutation(jax.random.fold_in(own, 1), rows)]
    turn = jax.random.randint(jax.random.fold_in(own, 2), (rows, 1), 0, top)
    return jnp.take_along_axis(table, (jnp.arange(top)[None, :] + turn) % top, axis=1)


def load_shares(amount, total, limit, skew, full):
    weights = [(1 << 20) // math.isqrt(standing ** skew) + 1 for standing in range(1, amount + 1)]
    largest = limit if full else min(limit, max(-(-total // amount), total * weights[0] // sum(weights)))
    least = 1 if total - largest >= amount - 1 else 0
    given, surplus = [largest] + [least] * (amount - 1), total - largest - least * (amount - 1)
    while surplus > 0:
        candidates = [i for i in range(1, amount) if given[i] < largest] or [i for i in range(1, amount) if given[i] < limit]
        whole, budget = sum([weights[i] for i in candidates]), surplus
        for i in candidates:
            more = min(limit - given[i], max(1, budget * weights[i] // whole), surplus)
            given[i] = given[i] + more
            surplus = surplus - more
    return np.array(given)


def bell_draw(own_key, shape, deviation, bound, pieces=(), kind=jnp.bfloat16):
    factor_of = block_levels(own_key, shape, pieces, -0.22, 0.18) if pieces else 1.0
    result = jax.random.normal(own_key, shape, jnp.float32) * deviation * factor_of
    return jnp.minimum(jnp.maximum(result, -bound), bound).astype(kind)


def setup_inputs(seed: int = 0) -> dict:
    key_list = jax.random.split(jax.random.key(seed), 14)
    species = jnp.clip(0.25 * jax.random.uniform(key_list[0], (NSPEC, NBLOCKS * CI, JK), jnp.float32) ** block_levels(key_list[0], (NSPEC, NBLOCKS * CI, JK), ((0, 4), (1, 64)), -0.2, 0.2), 0.0, 0.25)
    interface_normal_flow = bell_draw(key_list[1], (3, NBLOCKS * CI, JK), 1.0, 6.0, ((1, 64),), jnp.float32)
    face_diffusion = jnp.clip(jnp.exp(math.log(3.0) - 2.3025851 * jax.random.uniform(key_list[2], (3, NBLOCKS * CI, JK), jnp.float32) ** block_levels(key_list[2], (3, NBLOCKS * CI, JK), ((1, 64),), -0.2, 0.2)), 0.3, 3.0)
    inv_volume = jnp.clip(jnp.exp(math.log(2.0) - 1.3862944 * jax.random.uniform(key_list[3], (NBLOCKS * CI, JK), jnp.float32) ** block_levels(key_list[3], (NBLOCKS * CI, JK), ((0, 64),), -0.2, 0.2)), 0.5, 2.0)
    diffusivity = jnp.clip(jnp.exp(math.log(2.0) - 2.3025851 * jax.random.uniform(key_list[4], (NSPEC,), jnp.float32) ** block_levels(key_list[4], (NSPEC,), ((0, 4),), -0.2, 0.2)), 0.2, 2.0)
    low_partner = draw_low_partner(jax.random.fold_in(key_list[13], 71), 0)
    high_partner = draw_high_partner(jax.random.fold_in(key_list[13], 71), 0)
    low_orient = draw_low_orient(jax.random.fold_in(key_list[13], 71), 0)
    high_orient = draw_high_orient(jax.random.fold_in(key_list[13], 71), 0)
    droplet_table = bell_draw(key_list[9], (NBLOCKS * N_SP * PAR_DEV, PV), 1.0, 6.0, ((0, 256),), jnp.float32)
    parcel_block_keys = jax.random.split(jax.random.fold_in(key_list[10], 1), (NBLOCKS * N_SP * PAR_DEV) // PAR_DEV)
    parcel_block_turns = jax.random.permutation(jax.random.fold_in(key_list[10], 3), (NBLOCKS * N_SP * PAR_DEV) // PAR_DEV)
    parcel_block = jax.vmap(lambda own, number: assign_block(jax.random.fold_in(key_list[10], 2), own, number, PAR_DEV, NBLOCKS, 1, PCAP, 2))(parcel_block_keys, parcel_block_turns).reshape((NBLOCKS * N_SP * PAR_DEV, 1))
    parcel_cell = set_ends(jax.random.randint(key_list[11], (NBLOCKS * N_SP * PAR_DEV,), 0, CI * JK), jax.random.fold_in(key_list[11], 1), 0, (CI * JK) - 1).astype(jnp.int32)
    parcel_live = set_ends((jax.random.randint(key_list[12], (NBLOCKS * N_SP * PAR_DEV,), 0, 4) < 3).astype(jnp.int32), jax.random.fold_in(key_list[12], 1), 0, 1)
    return dict(species=species, interface_normal_flow=interface_normal_flow, face_diffusion=face_diffusion, inv_volume=inv_volume, diffusivity=diffusivity, low_partner=low_partner, high_partner=high_partner, low_orient=low_orient, high_orient=high_orient, droplet_table=droplet_table, parcel_block=parcel_block, parcel_cell=parcel_cell, parcel_live=parcel_live)


section_step = 0.5
friction_timescale = 0.3


def face_tiles(face):
    leading = face.shape[:-1]
    levels = len(leading)
    blocked = face.reshape(leading + (BJ // TILE_SIDE, TILE_SIDE, BK // TILE_SIDE, TILE_SIDE))
    axes_order = tuple(range(levels)) + (levels, levels + 2, levels + 1, levels + 3)
    return jnp.transpose(blocked, axes_order).reshape(leading + (TILES, TILE_SIDE * TILE_SIDE))


def tile_face(tiles):
    leading = tiles.shape[:-2]
    levels = len(leading)
    blocked = tiles.reshape(leading + (BJ // TILE_SIDE, BK // TILE_SIDE, TILE_SIDE, TILE_SIDE))
    axes_order = tuple(range(levels)) + (levels, levels + 2, levels + 1, levels + 3)
    return jnp.transpose(blocked, axes_order).reshape(leading + (BJ * BK,))


def orient(tiles, codes, inverse):
    square = tiles.reshape(tiles.shape[:-1] + (TILE_SIDE, TILE_SIDE))
    selector = codes[..., None, None, None]
    transposed = (selector // 4) % 2 == 1
    flip_rows = selector % 2 == 1
    flip_columns = (selector // 2) % 2 == 1
    if not inverse:
        square = jnp.where(transposed, jnp.swapaxes(square, -1, -2), square)
    square = jnp.where(flip_rows, jnp.flip(square, -2), square)
    square = jnp.where(flip_columns, jnp.flip(square, -1), square)
    if inverse:
        square = jnp.where(transposed, jnp.swapaxes(square, -1, -2), square)
    return square.reshape(tiles.shape)


def face_terms(ghost_low, values, ghost_high):
    extended = jnp.concatenate([ghost_low[:, None], values, ghost_high[:, None]], axis=1)
    upper_side = extended[:, 1:]
    lower_side = extended[:, :-1]
    previous_row = jnp.roll(values, BK, axis=-1)
    previous_column = jnp.roll(values, 1, axis=-1)
    differences = (upper_side - lower_side, values - previous_row, values - previous_column)
    averages = (0.5 * (upper_side + lower_side), 0.5 * (values + previous_row), 0.5 * (values + previous_column))
    return differences, averages


def partial_weights(differences, diffusivity):
    scaled = diffusivity[:, None, None]
    return tuple(jnp.sum(scaled * difference, axis=0) for difference in differences)


def advance(values, differences, averages, weights, velocity_faces, diffusion_faces, diffusivity, inv_volume, source, is_fuel):
    scaled = diffusivity[:, None, None]
    cell_index = jnp.arange(BJ * BK)
    wall_rows = cell_index // BK == 0
    wall_columns = cell_index % BK == 0
    fluxes = []
    for difference, middle, weight, velocity, diffusion in zip(differences, averages, weights, velocity_faces, diffusion_faces):
        fluxes.append(velocity * middle - diffusion * (scaled * difference - middle * weight))
    flux_layer, flux_row, flux_column = fluxes
    flux_row = jnp.where(wall_rows, 0.0, flux_row)
    flux_column = jnp.where(wall_columns, 0.0, flux_column)
    divergence = (flux_layer[:, 1:] - flux_layer[:, :-1]) + (jnp.roll(flux_row, -BK, axis=-1) - flux_row) + (jnp.roll(flux_column, -1, axis=-1) - flux_column)
    tendency = inv_volume * (source * (is_fuel - values) - divergence)
    return values + section_step * tendency


def droplet_motion_update(droplet_table, evaporate_component, ambient_flow_speed, alive_indicator):
    boiled_off_quantity = jax.nn.softplus(droplet_table[:, 1]) * (jax.nn.sigmoid(droplet_table[:, 2]) - evaporate_component) * alive_indicator
    shifted_droplet_list = droplet_table.at[:, 0].add(-boiled_off_quantity)
    shifted_droplet_list = shifted_droplet_list.at[:, 3:6].add(friction_timescale * (jnp.transpose(ambient_flow_speed) - droplet_table[:, 3:6]))
    return boiled_off_quantity, shifted_droplet_list * alive_indicator[:, None]


def reference(species, interface_normal_flow, face_diffusion, inv_volume, diffusivity, low_partner, high_partner, low_orient, high_orient, droplet_table, parcel_block, parcel_cell, parcel_live):
    spec_blocks = species.reshape(NSPEC, NBLOCKS, CI, BJ * BK)
    velocity_blocks = interface_normal_flow.reshape(3, NBLOCKS, CI, BJ * BK)
    diffusion_blocks = face_diffusion.reshape(3, NBLOCKS, CI, BJ * BK)
    high_tiles = jnp.transpose(face_tiles(spec_blocks[:, :, CI - 1]), (1, 2, 0, 3))
    low_face = jnp.concatenate([spec_blocks[:, :, 0], velocity_blocks[0:1, :, 0], diffusion_blocks[0:1, :, 0]], axis=0)
    low_tiles = jnp.transpose(face_tiles(low_face), (1, 2, 0, 3))
    tile_number = jnp.arange(TILES)[None, :]
    picked_high = high_tiles[low_partner, tile_number]
    ghost_low = tile_face(jnp.transpose(orient(picked_high, low_orient, False), (0, 2, 1, 3)))
    picked_low = low_tiles[high_partner, tile_number]
    ghost_high = tile_face(jnp.transpose(orient(picked_low, high_orient, True), (0, 2, 1, 3)))

    device_count = NBLOCKS * N_SP
    total_rows = device_count * PAR_DEV
    row_number = jnp.arange(total_rows, dtype=jnp.int32)
    source_device = row_number // PAR_DEV
    source_block = source_device // N_SP
    source_group = source_device % N_SP
    target_block = parcel_block[:, 0]
    active_rows = parcel_live == 1
    onehot = ((target_block[:, None] == jnp.arange(NBLOCKS, dtype=jnp.int32)[None, :]) & active_rows[:, None]).astype(jnp.int32)
    onehot = onehot.reshape(device_count, PAR_DEV, NBLOCKS)
    before = jnp.cumsum(onehot, axis=1) - onehot
    rank_before = jnp.sum(before * onehot, axis=-1).reshape(total_rows)
    arrival_rows = NBLOCKS * N_SP * NBLOCKS * PCAP
    slot_index = ((target_block * N_SP + source_group) * NBLOCKS + source_block) * PCAP + rank_before
    slot_index = jnp.where(active_rows, slot_index, arrival_rows).astype(jnp.int32)
    overall_grid_number = (target_block * (CI * BJ * BK) + parcel_cell).astype(jnp.int32)
    evaporate_component = species[0].reshape(-1)[overall_grid_number]
    ambient_flow_speed = interface_normal_flow.reshape(3, -1)[:, overall_grid_number]
    alive_indicator = active_rows.astype(jnp.float32)
    boiled_off_quantity, shifted_droplet_list = droplet_motion_update(droplet_table, evaporate_component, ambient_flow_speed, alive_indicator)
    arrived = jnp.zeros((arrival_rows, PV), jnp.float32).at[slot_index].set(shifted_droplet_list, mode="drop")
    source = jnp.zeros((NBLOCKS * CI * BJ * BK,), jnp.float32).at[overall_grid_number].add(boiled_off_quantity)
    source = source.reshape(NBLOCKS, CI, BJ * BK)

    is_fuel = (jnp.arange(NSPEC) == 0).astype(jnp.float32)[:, None, None]

    def one_block(inputs):
        values, velocity, diffusion, volume, low_side, high_side, block_source = inputs
        differences, averages = face_terms(low_side, values, high_side[:NSPEC])
        weights = partial_weights(differences, diffusivity)
        velocity_faces = (jnp.concatenate([velocity[0], high_side[NSPEC:NSPEC + 1]], axis=0), velocity[1], velocity[2])
        diffusion_faces = (jnp.concatenate([diffusion[0], high_side[NSPEC + 1:NSPEC + 2]], axis=0), diffusion[1], diffusion[2])
        return advance(values, differences, averages, weights, velocity_faces, diffusion_faces, diffusivity, volume, block_source, is_fuel)

    updated = lax.map(one_block, (jnp.transpose(spec_blocks, (1, 0, 2, 3)), jnp.transpose(velocity_blocks, (1, 0, 2, 3)), jnp.transpose(diffusion_blocks, (1, 0, 2, 3)), inv_volume.reshape(NBLOCKS, CI, BJ * BK), ghost_low, ghost_high, source))
    new_species = jnp.transpose(updated, (1, 0, 2, 3)).reshape(NSPEC, NBLOCKS * CI, BJ * BK)
    return new_species, arrived
```

```python
import functools
import jax
import jax.numpy as jnp
import numpy as np
from jax import lax
from jax.experimental import pallas as pl
from jax.experimental.pallas import tpu as pltpu
from jax.sharding import PartitionSpec as P

NB = 64
NQ = 4
CAP = 6
LAYERS = 32
JK = 4096
MESH = pl.DeviceIdType.MESH
F32 = jnp.float32
BF16 = jnp.bfloat16
STEP = 0.5
DRAG = 0.3
VMEM_LIMIT = 48 * 1024 * 1024


def constants():
    lane = np.arange(512)
    cell = np.arange(64)
    pick = (lane[:, None] // 64 == cell[None, :] // 8) & (lane[:, None] % 8 == cell[None, :] % 8)
    r, c = cell // 8, cell % 8
    oriented, unoriented = [], []
    for code in range(8):
        f_row = (lambda v: 7 - v) if code & 1 else (lambda v: v)
        f_col = (lambda v: 7 - v) if code & 2 else (lambda v: v)
        r2, c2 = f_row(r), f_col(c)
        source = c2 * 8 + r2 if code & 4 else r2 * 8 + c2
        oriented += [cell[:, None] == source[None, :]] * 2
        source = f_row(c) * 8 + f_col(r) if code & 4 else f_row(r) * 8 + f_col(c)
        unoriented += [cell[:, None] == source[None, :]] * 2
    spread = np.zeros((128, 1024), bool)
    spread[:64, :512] = pick.T
    spread[64:, 512:] = pick.T
    asb = lambda m: jnp.asarray(m.astype(np.float32), BF16)
    return asb(pick), asb(np.concatenate(oriented, 1)), asb(np.concatenate(unoriented, 1)), asb(spread)


def pieces(x):
    hi = x.astype(BF16)
    rest = x - hi.astype(F32)
    mid = rest.astype(BF16)
    low = (rest - mid.astype(F32)).astype(BF16)
    return hi, mid, low


def mm(a, b):
    return lax.dot_general(a, b, (((1,), (0,)), ((), ())), preferred_element_type=F32)


def pick_rows(onehot, x):
    hi, mid, low = pieces(x)
    return (mm(onehot, hi) + mm(onehot, mid)) + mm(onehot, low)


def pick_lanes(x, onehot):
    hi, mid, low = pieces(x)
    return (mm(hi, onehot) + mm(mid, onehot)) + mm(low, onehot)


def iota(shape, axis):
    return lax.broadcasted_iota(jnp.int32, shape, axis)


def ones(mask):
    return jnp.where(mask, 1.0, 0.0).astype(BF16)


def column(row):
    n = row.shape[1]
    return jnp.sum(jnp.where(iota((n, n), 0) == iota((n, n), 1), row, 0.0), axis=1, keepdims=True)


def strip_mask():
    lane = iota((8, 512), 1)
    return (lane % 64) // 8 == iota((8, 512), 0)


def prep_kernel(
    dif, species, flow, diffusion, low_partner, high_partner, low_orient, high_orient,
    table, block, cell, live, pick, oriented, unoriented, msg_a, msg_b, z_part,
):
    d0, d1 = dif[0], dif[1]
    z_part[...] = d0 * species[0] + d1 * species[1]

    n = table.shape[0]
    alive = live[...] == 1
    target = block[...].astype(F32)
    key = jnp.where(alive, target, -1.0)
    key_col = column(key)
    same = key_col == key
    first, second = iota((n, n), 0), iota((n, n), 1)
    rank = jnp.sum(jnp.where(same & (first < second), 1.0, 0.0), axis=0, keepdims=True)
    rank_col = jnp.sum(jnp.where(same & (second < first), 1.0, 0.0), axis=1, keepdims=True)
    slot = jnp.where(alive, target * CAP + rank, -1.0)
    rows = table[...]
    place = ones(iota((NB * CAP, n), 0).astype(F32) == slot)
    msg_b[...] = pick_rows(place, rows)

    lane = iota((n, 128), 1)
    cell_col = column(cell[...].astype(F32))
    boil = jnp.maximum(rows, 0.0) + jnp.log1p(jnp.exp(-jnp.abs(rows)))
    sig = 1.0 / (1.0 + jnp.exp(-rows))
    kind = lane & 7
    meta = jnp.where(kind == 0, cell_col, jnp.where(kind == 1, boil[:, 1:2], jnp.where(kind == 2, sig[:, 2:3], jnp.where(kind == 3, 1.0, 0.0))))
    meta = jnp.where((lane >> 3).astype(F32) == rank_col, meta, 0.0)

    mask = strip_mask()
    faces = [
        species[0, LAYERS - 1 : LAYERS, :], species[1, LAYERS - 1 : LAYERS, :],
        species[0, 0:1, :], species[1, 0:1, :], flow[0, 0:1, :], diffusion[0, 0:1, :],
    ]
    strips = []
    for face in faces:
        for jt in range(8):
            strips.append(jnp.where(mask, face[:, jt * 512 : (jt + 1) * 512], 0.0))
    tiles = pick_lanes(jnp.concatenate(strips, axis=0), pick[...])
    turned = pick_lanes(tiles[:128], oriented[...])
    unturned = pick_lanes(tiles[128:], unoriented[...])
    high_code = column(high_orient[...].astype(F32))
    low_code = column(low_orient[...].astype(F32))

    def choose(x, code):
        out = x[:, :128]
        for o in range(1, 8):
            out = jnp.where(code == o, x[:, o * 128 : (o + 1) * 128], out)
        return out

    up0, up1 = (choose(turned[k * 64 : (k + 1) * 64], high_code) for k in range(2))
    lo0, lo1, fl, df = (choose(unturned[k * 64 : (k + 1) * 64], low_code) for k in range(4))
    left = iota((NB, 128), 1) < 64
    values = jnp.concatenate(
        [
            meta,
            jnp.where(left, up0, up1),
            jnp.where(left, lo0, lo1),
            jnp.where(left, fl, df),
            jnp.where(left, d0 * up0 + d1 * up1, 0.0),
            jnp.where(left, 0.0, d0 * lo0 + d1 * lo1),
        ],
        axis=0,
    )
    hp, lp = high_partner[...].astype(F32) * CAP, low_partner[...].astype(F32) * CAP
    keys = jnp.concatenate([jnp.where(alive, target * CAP, -1.0), hp + 2.0, lp + 3.0, lp + 4.0, hp + 1.0, lp + 1.0], axis=1)
    where_to = ones(iota((NB * CAP, keys.shape[1]), 0).astype(F32) == keys)
    msg_a[...] = pick_rows(where_to, values)


def exchange_kernel(msg_a, msg_b, z_part, recv_a, recv_b, z_sum, forward, z_got, z_mine, z_own, sems, recv_sems, wide_send, wide_recv, local_sems):
    b, q = lax.axis_index("blk"), lax.axis_index("sp")
    barrier = pltpu.get_barrier_semaphore()

    def greet(i, carry):
        pl.semaphore_signal(barrier, inc=1, device_id=(lax.rem(b + i, NB), q), device_id_type=MESH)
        return carry

    for d in range(1, NQ):
        pl.semaphore_signal(barrier, inc=1, device_id=(b, lax.rem(q + d, NQ)), device_id_type=MESH)
    lax.fori_loop(1, NB, greet, 0)
    own = pltpu.make_async_copy(z_part.at[q], z_own, local_sems.at[0])
    own.start()
    keep_a = pltpu.make_async_copy(msg_a.at[b], recv_a.at[b], local_sems.at[1])
    keep_b = pltpu.make_async_copy(msg_b.at[b], recv_b.at[b], local_sems.at[2])
    keep_a.start()
    keep_b.start()
    pl.semaphore_wait(barrier, NB + NQ - 2)

    def sp_copy(src, dst, k, d):
        return pltpu.make_async_remote_copy(
            src_ref=src, dst_ref=dst, send_sem=sems.at[k, d - 1], recv_sem=recv_sems.at[k, d - 1],
            device_id=(b, lax.rem(q + d, NQ)), device_id_type=MESH,
        )

    scatter = [sp_copy(z_part.at[lax.rem(q + d, NQ)], z_got.at[d - 1], 0, d) for d in range(1, NQ)]
    for copy in scatter:
        copy.start()

    def send(msg, recv, k):
        def step(i, carry):
            to = lax.rem(b + i, NB)
            pltpu.make_async_remote_copy(
                src_ref=msg.at[to], dst_ref=recv.at[b], send_sem=wide_send.at[k], recv_sem=wide_recv.at[k],
                device_id=(to, q), device_id_type=MESH,
            ).start()
            return carry

        lax.fori_loop(1, NB, step, 0)

    send(msg_a, recv_a, 0)
    send(msg_b, recv_b, 1)

    own.wait()
    for copy in scatter:
        copy.wait_recv()
    z_mine[...] = (z_own[...] + z_got[0]) + (z_got[1] + z_got[2])
    gather = [sp_copy(z_mine, z_sum.at[q], 1, d) for d in range(1, NQ)]
    for copy in gather:
        copy.start()
    keep_z = pltpu.make_async_copy(z_mine, z_sum.at[q], local_sems.at[3])
    keep_z.start()

    keep_a.wait()
    most = pl.ds(0, NB - 1)
    pltpu.make_async_copy(recv_a.at[most], recv_a.at[most], wide_recv.at[0]).wait()
    onward = [sp_copy(recv_a.at[:, 0], forward.at[q], 2, d) for d in range(1, NQ)]
    for copy in onward:
        copy.start()
    keep_f = pltpu.make_async_copy(recv_a.at[:, 0], forward.at[q], local_sems.at[4])
    keep_f.start()

    keep_b.wait()
    keep_z.wait()
    keep_f.wait()
    pltpu.make_async_copy(recv_b.at[most], recv_b.at[most], wide_recv.at[1]).wait()
    pltpu.make_async_copy(msg_a.at[most], msg_a.at[most], wide_send.at[0]).wait()
    pltpu.make_async_copy(msg_b.at[most], msg_b.at[most], wide_send.at[1]).wait()
    for copy in scatter:
        copy.wait_send()
    for copy in gather + onward:
        copy.wait()


def stack_field(ref_slice):
    return jnp.concatenate([ref_slice[:, i * 128 : (i + 1) * 128] for i in range(LAYERS)], axis=0)


def lookup(cells, field3):
    n = cells.shape[0]
    whole = cells.astype(jnp.int32)
    row = ((whole & 4095) >> 7) * LAYERS + (whole >> 12)
    got = mm(ones(iota((n, 1024), 1) == row), field3)
    got = (got[:, :128] + got[:, 128:256]) + got[:, 256:]
    return jnp.sum(jnp.where(iota((n, 128), 1) == (whole & 127), got, 0.0), axis=1, keepdims=True)


def fuel_kernel(forward, fuel, out):
    field3 = jnp.concatenate(pieces(stack_field(fuel[0])), axis=1)
    meta = forward[pl.ds(0, NB * NQ, stride=2), :]
    lane = iota((NB * NQ, 128), 1)
    found = jnp.zeros((NB * NQ, 128), F32)
    for r in range(CAP):
        found = jnp.where(lane == r, lookup(meta[:, 8 * r : 8 * r + 1], field3), found)
    out[...] = jnp.transpose(found)[:8]


def share_kernel(mine, out, sems, recv_sems, local_sem):
    b, q = lax.axis_index("blk"), lax.axis_index("sp")
    barrier = pltpu.get_barrier_semaphore()
    for d in range(1, NQ):
        pl.semaphore_signal(barrier, inc=1, device_id=(b, lax.rem(q + d, NQ)), device_id_type=MESH)
    pl.semaphore_wait(barrier, NQ - 1)

    @pl.when(q == 0)
    def _():
        keep = pltpu.make_async_copy(mine, out, local_sem)
        keep.start()
        copies = [
            pltpu.make_async_remote_copy(
                src_ref=mine, dst_ref=out, send_sem=sems.at[d - 1], recv_sem=recv_sems, device_id=(b, d), device_id_type=MESH
            )
            for d in range(1, NQ)
        ]
        for copy in copies:
            copy.start()
        for copy in copies:
            copy.wait_send()
        keep.wait()

    @pl.when(q != 0)
    def _():
        pltpu.make_async_copy(mine, out, recv_sems).wait()


def final_kernel(
    dif, species, flow, diffusion, inv_volume, z_sum, low_partner, high_partner,
    recv_a, recv_b, forward, found, spread, new_species, arrived, ghosts, source, fuel_col,
):
    q = lax.axis_index("sp")
    d = (dif[0], dif[1])
    left = iota((NB, 128), 1) < 64

    meta = forward[pl.ds(0, NB * NQ, stride=2), :]
    meta_t = jnp.transpose(meta)
    pad = jnp.concatenate([found[...], jnp.zeros((120, NB * NQ), F32)], axis=0)
    found_col = jnp.transpose(pad)
    fuel_col[...] = found_col
    lane = iota((NB * NQ, 128), 1)
    mass, cells = [], []
    for r in range(CAP):
        k = 8 * r
        gone = meta[:, k + 1 : k + 2] * (meta[:, k + 2 : k + 3] - found_col[:, r : r + 1])
        at = meta[:, k : k + 1].astype(jnp.int32) & 127
        mass.append(jnp.concatenate(pieces(jnp.where(lane == at, gone, 0.0)), axis=1))
        cells.append(meta_t[k : k + 1, :].astype(jnp.int32))
    mass = jnp.concatenate(mass, axis=0)
    cells = jnp.concatenate(cells, axis=1)
    row = ((cells & 4095) >> 7) * LAYERS + (cells >> 12)
    for m in range(4):
        hot = ones(iota((256, NB * NQ * CAP), 0) + m * 256 == row)
        part = mm(hot, mass)
        source[m * 256 : (m + 1) * 256, :] = (part[:, :128] + part[:, 128:256]) + part[:, 256:]

    own = recv_a[pl.ds(0, NB, stride=6), :]
    own_cells = jnp.concatenate([own[:, 8 * r : 8 * r + 1] for r in range(CAP)], axis=0)
    speeds = [lookup(own_cells, jnp.concatenate(pieces(stack_field(flow[k])), axis=1)) for k in range(3)]
    own_fuel = fuel_col[pl.ds(pl.multiple_of(q * NB, NB), NB), :]
    lane = iota((NB, 128), 1)
    keep = jnp.where((lane >= 3) & (lane <= 5), 1.0 - DRAG, 1.0)
    for r in range(CAP):
        k = 8 * r
        gone = own[:, k + 1 : k + 2] * (own[:, k + 2 : k + 3] - own_fuel[:, r : r + 1])
        drag = DRAG * own[:, k + 3 : k + 4]
        change = jnp.where(lane == 0, -gone, 0.0)
        for c in range(3):
            change = jnp.where(lane == 3 + c, drag * speeds[c][r * NB : (r + 1) * NB], change)
        arrived[pl.ds(r, NB, stride=CAP), :] = recv_b[pl.ds(r, NB, stride=CAP), :] * keep + change

    low_sel = ones(iota((NB, NB), 1).astype(F32) == column(low_partner[...].astype(F32)))
    high_sel = ones(iota((NB, NB), 1).astype(F32) == column(high_partner[...].astype(F32)))
    z_tiles = forward[pl.ds(1, NB * NQ, stride=2), :]
    z_tiles = (z_tiles[:64] + z_tiles[64:128]) + (z_tiles[128:192] + z_tiles[192:])
    below = pick_rows(low_sel, jnp.concatenate([recv_a[pl.ds(2, NB, stride=6), :], z_tiles], axis=1))
    above = pick_rows(high_sel, jnp.concatenate([recv_a[pl.ds(3, NB, stride=6), :], recv_a[pl.ds(4, NB, stride=6), :], z_tiles], axis=1))
    tiles = jnp.concatenate([below[:, :128], above[:, :128], above[:, 128:256], jnp.where(left, below[:, 128:], above[:, 256:])], axis=0)
    wide = pick_lanes(tiles, spread[...])
    mask = strip_mask()
    slots = ((0, 1), (3, 4), (6, 7), (2, 5))
    for g in range(4):
        for jt in range(8):
            block = wide[g * 64 + jt * 8 : g * 64 + jt * 8 + 8]
            for half in range(2):
                value = jnp.sum(jnp.where(mask, block[:, half * 512 : (half + 1) * 512], 0.0), axis=0, keepdims=True)
                ghosts[slots[g][half] : slots[g][half] + 1, jt * 512 : (jt + 1) * 512] = value

    lane = iota((LAYERS, 128), 1)
    layer = iota((LAYERS, 128), 0)
    fuel = jnp.where(q == 0, 1.0, 0.0)
    right_half = lane >= 64
    inside = (lane & 63) != 0

    def strip(n, carry):
        i = LAYERS - 1 - n
        here = pl.ds(pl.multiple_of(i * 128, 128), 128)
        back = pl.ds(pl.multiple_of(jnp.maximum(i - 1, 0) * 128, 128), 128)
        beyond_wall = (i > 0) | right_half

        def below_of(x, ghost):
            return jnp.where(layer == 0, ghost, pltpu.roll(x, 1, 0))

        def before_of(x, previous):
            return pltpu.roll(jnp.where(right_half, previous, x), 64, 1)

        z = z_sum[:, here]
        g0, g1, g2 = diffusion[0, :, here], diffusion[1, :, here], diffusion[2, :, here]
        gt = ghosts[7:8, here]
        h0 = 0.5 * (flow[0, :, here] + g0 * (z - below_of(z, ghosts[2:3, here])))
        ht = 0.5 * (ghosts[6:7, here] + gt * (ghosts[5:6, here] - z[LAYERS - 1 :]))
        h1 = 0.5 * (flow[1, :, here] + g1 * (z - before_of(z, z_sum[:, back])))
        h2 = 0.5 * (flow[2, :, here] + g2 * (z - pltpu.roll(z, 1, 1)))
        h1, g1 = jnp.where(beyond_wall, h1, 0.0), jnp.where(beyond_wall, g1, 0.0)
        h2, g2 = jnp.where(inside, h2, 0.0), jnp.where(inside, g2, 0.0)
        half_inv = STEP * inv_volume[:, here]
        src = source[pl.ds(pl.multiple_of(i * LAYERS, LAYERS), LAYERS), :]
        out = []
        for s in range(2):
            y = species[s, :, here]
            top = ghosts[3 + s : 4 + s, here]
            last = y[LAYERS - 1 :]
            y0 = below_of(y, ghosts[s : s + 1, here])
            y1 = before_of(y, species[s, :, back])
            y2 = pltpu.roll(y, 1, 1)
            f0 = h0 * (y + y0) - (g0 * d[s]) * (y - y0)
            ft = ht * (top + last) - (gt * d[s]) * (top - last)
            f1 = h1 * (y + y1) - (g1 * d[s]) * (y - y1)
            f2 = h2 * (y + y2) - (g2 * d[s]) * (y - y2)
            u0 = jnp.where(layer == LAYERS - 1, ft, pltpu.roll(f0, LAYERS - 1, 0))
            u1 = pltpu.roll(jnp.where(right_half, f1, carry[s]), 64, 1)
            u2 = pltpu.roll(f2, 127, 1)
            divergence = (u0 - f0) + ((u1 - f1) + (u2 - f2))
            delta = fuel if s == 0 else 0.0
            new_species[s, :, here] = y + half_inv * (src * (delta - y) - divergence)
            out.append(f1)
        return tuple(out)

    lax.fori_loop(0, LAYERS, strip, (jnp.zeros((LAYERS, 128), F32),) * 2)


def spec(space=pltpu.VMEM):
    return pl.BlockSpec(memory_space=space)


ANY = pl.BlockSpec(memory_space=pl.ANY)


def params(**kw):
    return pltpu.CompilerParams(vmem_limit_bytes=VMEM_LIMIT, **kw)


def shape(*dims):
    return jax.ShapeDtypeStruct(dims, F32)


def body(
    species, interface_normal_flow, face_diffusion, inv_volume, diffusivity, low_partner, high_partner,
    low_orient, high_orient, droplet_table, parcel_block, parcel_cell, parcel_live,
):
    pick, oriented, unoriented, spread = constants()
    first = pl.BlockSpec((1, 8, JK), lambda i: (0, 0, 0))
    whole = lambda *dims: pl.BlockSpec(dims, lambda i: (0,) * len(dims))
    msg_a, msg_b, z_part = pl.pallas_call(
        prep_kernel,
        grid=(1,),
        out_shape=(shape(384, 128), shape(384, 128), shape(LAYERS, JK)),
        in_specs=[
            pl.BlockSpec(memory_space=pltpu.SMEM), whole(2, LAYERS, JK), first, first,
            *[whole(1, 64)] * 4, whole(256, 128), *[whole(1, 256)] * 3,
            whole(512, 64), whole(64, 1024), whole(64, 1024),
        ],
        out_specs=(whole(384, 128), whole(384, 128), whole(LAYERS, JK)),
        compiler_params=params(),
        name="prep",
    )(
        diffusivity, species, interface_normal_flow, face_diffusion, low_partner, high_partner, low_orient, high_orient,
        droplet_table, parcel_block.reshape(1, -1), parcel_cell.reshape(1, -1), parcel_live.reshape(1, -1),
        pick, oriented, unoriented,
    )
    dma = pltpu.SemaphoreType.DMA
    recv_a, recv_b, z_sum, forward = pl.pallas_call(
        exchange_kernel,
        out_shape=(shape(NB, 3, 2, 128), shape(NB, 3, 2, 128), shape(NQ, 8, JK), shape(NQ, NB, 2, 128)),
        in_specs=[ANY] * 3,
        out_specs=(ANY,) * 4,
        scratch_shapes=[
            pltpu.VMEM((3, 8, JK), F32), pltpu.VMEM((8, JK), F32), pltpu.VMEM((8, JK), F32),
            dma((3, 3)), dma((3, 3)), dma((2,)), dma((2,)), dma((5,)),
        ],
        compiler_params=params(collective_id=0, has_side_effects=True),
        name="exchange",
    )(msg_a.reshape(NB, 3, 2, 128), msg_b.reshape(NB, 3, 2, 128), z_part.reshape(NQ, 8, JK))
    forward = forward.reshape(NQ * NB * 2, 128)
    mine = pl.pallas_call(
        fuel_kernel,
        grid=(1,),
        out_shape=shape(8, NB * NQ),
        in_specs=[whole(NQ * NB * 2, 128), whole(1, LAYERS, JK)],
        out_specs=whole(8, NB * NQ),
        compiler_params=params(),
        name="fuel",
    )(forward, species)
    found = pl.pallas_call(
        share_kernel,
        out_shape=shape(8, NB * NQ),
        in_specs=[ANY],
        out_specs=ANY,
        scratch_shapes=[dma((3,)), dma, dma],
        compiler_params=params(collective_id=1, has_side_effects=True),
        name="share",
    )(mine)
    new_species, arrived = pl.pallas_call(
        final_kernel,
        out_shape=(shape(2, LAYERS, JK), shape(384, 128)),
        in_specs=[pl.BlockSpec(memory_space=pltpu.SMEM)] + [spec()] * 12,
        out_specs=(spec(), spec()),
        scratch_shapes=[pltpu.VMEM((8, JK), F32), pltpu.VMEM((1024, 128), F32), pltpu.VMEM((256, 128), F32)],
        compiler_params=params(),
        name="final",
    )(
        diffusivity, species, interface_normal_flow, face_diffusion, inv_volume, z_sum.reshape(LAYERS, JK),
        low_partner, high_partner, recv_a.reshape(384, 128), recv_b.reshape(384, 128), forward, found, spread,
    )
    return new_species, arrived


def solution(mesh):
    placed = (
        P("sp", "blk", None), P(None, "blk", None), P(None, "blk", None), P("blk", None), P("sp"),
        P("blk", None), P("blk", None), P("blk", None), P("blk", None),
        P(("blk", "sp"), None), P(("blk", "sp"), None), P(("blk", "sp")), P(("blk", "sp")),
    )
    return jax.shard_map(
        body, mesh=mesh, in_specs=placed, out_specs=(P("sp", "blk", None), P(("blk", "sp"), None)), check_vma=False,
    )
```

```python
import functools
import jax
import jax.numpy as jnp
import numpy as np
from jax import lax
from jax.experimental import pallas as pl
from jax.experimental.pallas import tpu as pltpu
from jax.sharding import PartitionSpec as P

NB = 64
NQ = 4
CAP = 6
ROWS = 8
CHUNKS = 2
LAYERS = 32
JK = 4096
MESH = pl.DeviceIdType.MESH
F32 = jnp.float32
BF16 = jnp.bfloat16
STEP = 0.5
DRAG = 0.3
VMEM_LIMIT = 36 * 1024 * 1024


def constants():
    lane = np.arange(512)
    cell = np.arange(64)
    pick = (lane[:, None] // 64 == cell[None, :] // 8) & (lane[:, None] % 8 == cell[None, :] % 8)
    r, c = cell // 8, cell % 8
    oriented, unoriented = [], []
    for code in range(8):
        f_row = (lambda v: 7 - v) if code & 1 else (lambda v: v)
        f_col = (lambda v: 7 - v) if code & 2 else (lambda v: v)
        r2, c2 = f_row(r), f_col(c)
        source = c2 * 8 + r2 if code & 4 else r2 * 8 + c2
        oriented += [cell[:, None] == source[None, :]] * 2
        source = f_row(c) * 8 + f_col(r) if code & 4 else f_row(r) * 8 + f_col(c)
        unoriented += [cell[:, None] == source[None, :]] * 2
    spread = np.zeros((128, 1024), bool)
    spread[:64, :512] = pick.T
    spread[64:, 512:] = pick.T
    asb = lambda m: jnp.asarray(m.astype(np.float32), BF16)
    return asb(pick), asb(np.concatenate(oriented, 1)), asb(np.concatenate(unoriented, 1)), asb(spread)


def pieces(x):
    hi = x.astype(BF16)
    rest = x - hi.astype(F32)
    mid = rest.astype(BF16)
    low = (rest - mid.astype(F32)).astype(BF16)
    return hi, mid, low


def mm(a, b):
    return lax.dot_general(a, b, (((1,), (0,)), ((), ())), preferred_element_type=F32)


def pick_rows(onehot, x):
    hi, mid, low = pieces(x)
    return (mm(onehot, hi) + mm(onehot, mid)) + mm(onehot, low)


def pick_lanes(x, onehot):
    hi, mid, low = pieces(x)
    return (mm(hi, onehot) + mm(mid, onehot)) + mm(low, onehot)


def iota(shape, axis):
    return lax.broadcasted_iota(jnp.int32, shape, axis)


def ones(mask):
    return jnp.where(mask, 1.0, 0.0).astype(BF16)


def column(row):
    n = row.shape[1]
    return jnp.sum(jnp.where(iota((n, n), 0) == iota((n, n), 1), row, 0.0), axis=1, keepdims=True)


def strip_mask():
    lane = iota((8, 512), 1)
    return (lane % 64) // 8 == iota((8, 512), 0)


def stack_field(ref_slice):
    return jnp.concatenate([ref_slice[:, i * 128 : (i + 1) * 128] for i in range(LAYERS)], axis=0)


def lookup(cells, field3):
    return lookups(cells, [field3])[0]


def lookups(cells, fields):
    n = cells.shape[0]
    whole = cells.astype(jnp.int32)
    row = ((whole & 4095) >> 7) * LAYERS + (whole >> 12)
    hot = ones(iota((n, 1024), 1) == row)
    here = iota((n, 128), 1) == (whole & 127)
    out = []
    for field3 in fields:
        got = mm(hot, field3)
        got = (got[:, :128] + got[:, 128:256]) + got[:, 256:]
        out.append(jnp.sum(jnp.where(here, got, 0.0), axis=1, keepdims=True))
    return out


def build_messages(
    d0, d1, species, flow, diffusion, low_partner, high_partner, low_orient, high_orient,
    table, block, cell, live, pick, oriented, unoriented, msg_a, msg_b,
):
    n = table.shape[0]
    alive = live[...] == 1
    target = block[...].astype(F32)
    key = jnp.where(alive, target, -1.0)
    key_col = column(key)
    same = key_col == key
    first, second = iota((n, n), 0), iota((n, n), 1)
    rank = jnp.sum(jnp.where(same & (first < second), 1.0, 0.0), axis=0, keepdims=True)
    rank_col = jnp.sum(jnp.where(same & (second < first), 1.0, 0.0), axis=1, keepdims=True)
    slot = jnp.where(alive, target * ROWS + rank, -1.0)
    rows = table[...]
    place = ones(iota((NB * ROWS, n), 0).astype(F32) == slot)
    msg_b[...] = pick_rows(place, rows)

    lane = iota((n, 128), 1)
    cell_col = column(cell[...].astype(F32))
    boil = jnp.maximum(rows, 0.0) + jnp.log1p(jnp.exp(-jnp.abs(rows)))
    sig = 1.0 / (1.0 + jnp.exp(-rows))
    kind = lane & 7
    meta = jnp.where(kind == 0, cell_col, jnp.where(kind == 1, boil[:, 1:2], jnp.where(kind == 2, sig[:, 2:3], jnp.where(kind == 3, 1.0, 0.0))))
    meta = jnp.where((lane >> 3).astype(F32) == rank_col, meta, 0.0)

    mask = strip_mask()
    faces = [
        species[0, LAYERS - 1 : LAYERS, :], species[1, LAYERS - 1 : LAYERS, :],
        species[0, 0:1, :], species[1, 0:1, :], flow[0, 0:1, :], diffusion[0:1, :],
    ]
    strips = []
    for face in faces:
        for jt in range(8):
            strips.append(jnp.where(mask, face[:, jt * 512 : (jt + 1) * 512], 0.0))
    tiles = pick_lanes(jnp.concatenate(strips, axis=0), pick[...])
    turned = pick_lanes(tiles[:128], oriented[...])
    unturned = pick_lanes(tiles[128:], unoriented[...])
    high_code = column(high_orient[...].astype(F32))
    low_code = column(low_orient[...].astype(F32))

    def choose(x, code):
        out = x[:, :128]
        for o in range(1, 8):
            out = jnp.where(code == o, x[:, o * 128 : (o + 1) * 128], out)
        return out

    up0, up1 = (choose(turned[k * 64 : (k + 1) * 64], high_code) for k in range(2))
    lo0, lo1, fl, df = (choose(unturned[k * 64 : (k + 1) * 64], low_code) for k in range(4))
    left = iota((NB, 128), 1) < 64
    values = jnp.concatenate(
        [
            meta,
            jnp.where(left, up0, up1),
            jnp.where(left, lo0, lo1),
            jnp.where(left, fl, df),
            jnp.where(left, d0 * up0 + d1 * up1, 0.0),
            jnp.where(left, 0.0, d0 * lo0 + d1 * lo1),
        ],
        axis=0,
    )
    hp, lp = high_partner[...].astype(F32) * ROWS, low_partner[...].astype(F32) * ROWS
    keys = jnp.concatenate([jnp.where(alive, target * ROWS, -1.0), hp + 2.0, lp + 3.0, lp + 4.0, hp + 1.0, lp + 1.0], axis=1)
    where_to = ones(iota((NB * ROWS, keys.shape[1]), 0).astype(F32) == keys)
    msg_a[...] = pick_rows(where_to, values)


def exchange_kernel(
    dif_in, species_in, flow_in, diffusion_in, lp_in, hp_in, lo_in, ho_in, table_in, block_in, cell_in, live_in,
    pick_in, oriented_in, unoriented_in, spread_in,
    z_sum, source, ghosts, parcels, change,
    dif, species, flow, diffusion, lp, hp, lo, ho, table, block, cell, live, pick, oriented, unoriented, spread,
    msg_a, msg_b, recv_a, forward, z_part, z_got, z_mine, fuel_mine, fuel, hot,
    load_sems, sems, recv_sems, wide_send, wide_recv, local_sems, fuel_send, fuel_recv,
):
    b, q = lax.axis_index("blk"), lax.axis_index("sp")
    loads = [
        pltpu.make_async_copy(src, dst, load_sems.at[k])
        for k, (src, dst) in enumerate(
            (
                (dif_in, dif), (species_in, species), (flow_in, flow), (diffusion_in.at[0, pl.ds(0, 8)], diffusion),
                (lp_in, lp), (hp_in, hp), (lo_in, lo), (ho_in, ho), (table_in, table), (block_in, block),
                (cell_in, cell), (live_in, live), (pick_in, pick), (oriented_in, oriented), (unoriented_in, unoriented),
                (spread_in, spread),
            )
        )
    ]
    for load in loads:
        load.start()
    barrier = pltpu.get_barrier_semaphore()

    def greet(i, carry):
        pl.semaphore_signal(barrier, inc=1, device_id=(lax.rem(b + i, NB), q), device_id_type=MESH)
        return carry

    for d in range(1, NQ):
        pl.semaphore_signal(barrier, inc=1, device_id=(b, lax.rem(q + d, NQ)), device_id_type=MESH)
    lax.fori_loop(1, NB, greet, 0)
    for load in loads:
        load.wait()

    d0, d1 = dif[0], dif[1]
    for k in range(NQ):
        z_part[k] = d0 * species[0, k * 8 : (k + 1) * 8] + d1 * species[1, k * 8 : (k + 1) * 8]
    build_messages(
        d0, d1, species, flow, diffusion, lp, hp, lo, ho, table, block, cell, live, pick, oriented, unoriented,
        msg_a.reshape(NB * ROWS, 128), msg_b.reshape(NB * ROWS, 128),
    )
    pl.semaphore_wait(barrier, NB + NQ - 2)

    def sp_copy(src, dst, k, d):
        return pltpu.make_async_remote_copy(
            src_ref=src, dst_ref=dst, send_sem=sems.at[k, d - 1], recv_sem=recv_sems.at[k, d - 1],
            device_id=(b, lax.rem(q + d, NQ)), device_id_type=MESH,
        )

    wide = JK // CHUNKS
    part = [pl.ds(c * wide, wide) for c in range(CHUNKS)]
    scatter = [
        [sp_copy(z_part.at[lax.rem(q + d, NQ), :, part[c]], z_got.at[d - 1, :, part[c]], c, d) for d in (2, 1, 3)]
        for c in range(CHUNKS)
    ]
    for copies in scatter:
        for copy in copies:
            copy.start()

    rows_a, rows_b = pl.ds(0, 5), pl.ds(0, CAP)
    keep_a = pltpu.make_async_copy(msg_a.at[b, rows_a], recv_a.at[b, rows_a], local_sems.at[0])
    keep_b = pltpu.make_async_copy(msg_b.at[b, rows_b], parcels.at[b, rows_b], local_sems.at[1])
    keep_a.start()
    keep_b.start()

    def send(msg, recv, rows, k, start, stop):
        def step(i, carry):
            to = lax.rem(b + i, NB)
            pltpu.make_async_remote_copy(
                src_ref=msg.at[to, rows], dst_ref=recv.at[b, rows], send_sem=wide_send.at[k], recv_sem=wide_recv.at[k],
                device_id=(to, q), device_id_type=MESH,
            ).start()
            return carry

        lax.fori_loop(start, stop, step, 0)

    send(msg_a, recv_a, rows_a, 0, 1, NB)
    gather = []
    for c in range(CHUNKS):
        for copy in scatter[c]:
            copy.wait_recv()
        z_mine[:, part[c]] = (z_part[q, :, part[c]] + z_got[0, :, part[c]]) + (z_got[1, :, part[c]] + z_got[2, :, part[c]])
        copies = [sp_copy(z_mine.at[:, part[c]], z_sum.at[q, :, part[c]], CHUNKS + c, d) for d in (2, 1, 3)]
        for copy in copies:
            copy.start()
        gather += copies
    z_sum[q] = z_mine[...]

    most = pl.ds(0, NB - 1)
    keep_a.wait()
    pltpu.make_async_copy(recv_a.at[most, rows_a], recv_a.at[most, rows_a], wide_recv.at[0]).wait()
    two = pl.ds(0, 2)
    onward = [sp_copy(recv_a.at[:, two], forward.at[q, :, two], 2 * CHUNKS, d) for d in (2, 1, 3)]
    for copy in onward:
        copy.start()
    keep_f = pltpu.make_async_copy(recv_a.at[:, two], forward.at[q, :, two], local_sems.at[2])
    keep_f.start()
    send(msg_b, parcels, rows_b, 1, 1, NB)

    got = recv_a.reshape(NB * ROWS, 128)
    seen = forward.reshape(NQ * NB * ROWS, 128)
    own = got[pl.ds(0, NB, stride=ROWS), :]
    own_cells = jnp.concatenate([own[:, 8 * r : 8 * r + 1] for r in range(CAP)], axis=0)

    keep_f.wait()
    for copy in onward:
        copy.wait_recv()
    meta = seen[pl.ds(0, NB * NQ, stride=ROWS), :]

    @pl.when(q == 0)
    def _():
        field3 = jnp.concatenate(pieces(stack_field(species[0])), axis=1)
        lane = iota((NB * NQ, 128), 1)
        found = jnp.zeros((NB * NQ, 128), F32)
        for r in range(CAP):
            found = jnp.where(lane == r, lookup(meta[:, 8 * r : 8 * r + 1], field3), found)
        fuel_mine[...] = jnp.transpose(found)[:8]
        copies = [
            pltpu.make_async_remote_copy(
                src_ref=fuel_mine, dst_ref=fuel, send_sem=fuel_send.at[d - 1], recv_sem=fuel_recv, device_id=(b, d), device_id_type=MESH
            )
            for d in (2, 1, 3)
        ]
        for copy in copies:
            copy.start()
        keep = pltpu.make_async_copy(fuel_mine, fuel, local_sems.at[3])
        keep.start()
        keep.wait()
        for copy in copies:
            copy.wait_send()

    meta_t = jnp.transpose(meta)
    cells = jnp.concatenate([meta_t[8 * r : 8 * r + 1, :] for r in range(CAP)], axis=1).astype(jnp.int32)
    row = ((cells & 4095) >> 7) * LAYERS + (cells >> 12)
    for m in range(4):
        hot[m * 256 : (m + 1) * 256, :] = ones(iota((256, NB * NQ * CAP), 0) + m * 256 == row)
    speeds = lookups(own_cells, [jnp.concatenate(pieces(stack_field(flow[k])), axis=1) for k in range(3)])

    low_sel = ones(iota((NB, NB), 1).astype(F32) == column(lp[...].astype(F32)))
    high_sel = ones(iota((NB, NB), 1).astype(F32) == column(hp[...].astype(F32)))
    z_tiles = seen[pl.ds(1, NB * NQ, stride=ROWS), :]
    z_tiles = (z_tiles[:64] + z_tiles[64:128]) + (z_tiles[128:192] + z_tiles[192:])
    left = iota((NB, 128), 1) < 64
    below = pick_rows(low_sel, jnp.concatenate([got[pl.ds(2, NB, stride=ROWS), :], z_tiles], axis=1))
    above = pick_rows(high_sel, jnp.concatenate([got[pl.ds(3, NB, stride=ROWS), :], got[pl.ds(4, NB, stride=ROWS), :], z_tiles], axis=1))
    tiles = jnp.concatenate([below[:, :128], above[:, :128], above[:, 128:256], jnp.where(left, below[:, 128:], above[:, 256:])], axis=0)
    spread_tiles = pick_lanes(tiles, spread[...])
    mask = strip_mask()
    slots = ((0, 1), (3, 4), (6, 7), (2, 5))
    for g in range(4):
        for jt in range(8):
            strip = spread_tiles[g * 64 + jt * 8 : g * 64 + jt * 8 + 8]
            for half in range(2):
                value = jnp.sum(jnp.where(mask, strip[:, half * 512 : (half + 1) * 512], 0.0), axis=0, keepdims=True)
                ghosts[slots[g][half] : slots[g][half] + 1, jt * 512 : (jt + 1) * 512] = value

    @pl.when(q != 0)
    def _():
        pltpu.make_async_copy(fuel_mine, fuel, fuel_recv).wait()

    found_col = jnp.transpose(jnp.concatenate([fuel[...], jnp.zeros((120, NB * NQ), F32)], axis=0))
    lane = iota((NB * NQ, 128), 1)
    mass = []
    for r in range(CAP):
        k = 8 * r
        gone = meta[:, k + 1 : k + 2] * (meta[:, k + 2 : k + 3] - found_col[:, r : r + 1])
        at = meta[:, k : k + 1].astype(jnp.int32) & 127
        mass.append(jnp.concatenate(pieces(jnp.where(lane == at, gone, 0.0)), axis=1))
    part3 = mm(hot[...], jnp.concatenate(mass, axis=0))
    source[...] = (part3[:, :128] + part3[:, 128:256]) + part3[:, 256:]

    group = iota((NB, NB * NQ), 1) - q * NB == iota((NB, NB * NQ), 0)
    own_fuel = pick_rows(ones(group), found_col)
    lane = iota((NB, 128), 1)
    for r in range(CAP):
        k = 8 * r
        gone = own[:, k + 1 : k + 2] * (own[:, k + 2 : k + 3] - own_fuel[:, r : r + 1])
        drag = DRAG * own[:, k + 3 : k + 4]
        moved = jnp.where(lane == 0, -gone, 0.0)
        for c in range(3):
            moved = jnp.where(lane == 3 + c, drag * speeds[c][r * NB : (r + 1) * NB], moved)
        change[pl.ds(r, NB, stride=CAP), :] = moved

    pltpu.make_async_copy(msg_a.at[most, rows_a], msg_a.at[most, rows_a], wide_send.at[0]).wait()
    pltpu.make_async_copy(msg_b.at[most, rows_b], msg_b.at[most, rows_b], wide_send.at[1]).wait()
    for copies in scatter:
        for copy in copies:
            copy.wait_send()
    for copy in onward:
        copy.wait_send()
    for copy in gather:
        copy.wait()
    keep_b.wait()
    pltpu.make_async_copy(parcels.at[most, rows_b], parcels.at[most, rows_b], wide_recv.at[1]).wait()


def final_kernel(
    dif, species, flow, diffusion, inv_volume, z_sum, source, ghosts, parcels, change, new_species, arrived, out, out_sems,
):
    q = lax.axis_index("sp")
    d = (dif[0], dif[1])
    lane = iota((NB, 128), 1)
    keep = jnp.where((lane >= 3) & (lane <= 5), 1.0 - DRAG, 1.0)
    for r in range(CAP):
        arrived[pl.ds(r, NB, stride=CAP), :] = parcels[pl.ds(r, NB, stride=ROWS), :] * keep + change[pl.ds(r, NB, stride=CAP), :]

    lane = iota((LAYERS, 128), 1)
    layer = iota((LAYERS, 128), 0)
    fuel = jnp.where(q == 0, 1.0, 0.0)
    right_half = lane >= 64
    inside = (lane & 63) != 0

    def strip(n, carry):
        i = LAYERS - 1 - n
        here = pl.ds(pl.multiple_of(i * 128, 128), 128)
        back = pl.ds(pl.multiple_of(jnp.maximum(i - 1, 0) * 128, 128), 128)
        beyond_wall = (i > 0) | right_half

        def below_of(x, ghost):
            return jnp.where(layer == 0, ghost, pltpu.roll(x, 1, 0))

        def before_of(x, previous):
            return pltpu.roll(jnp.where(right_half, previous, x), 64, 1)

        z = z_sum[:, here]
        g0, g1, g2 = diffusion[0, :, here], diffusion[1, :, here], diffusion[2, :, here]
        gt = ghosts[7:8, here]
        h0 = 0.5 * (flow[0, :, here] + g0 * (z - below_of(z, ghosts[2:3, here])))
        ht = 0.5 * (ghosts[6:7, here] + gt * (ghosts[5:6, here] - z[LAYERS - 1 :]))
        h1 = 0.5 * (flow[1, :, here] + g1 * (z - before_of(z, z_sum[:, back])))
        h2 = 0.5 * (flow[2, :, here] + g2 * (z - pltpu.roll(z, 1, 1)))
        h1, g1 = jnp.where(beyond_wall, h1, 0.0), jnp.where(beyond_wall, g1, 0.0)
        h2, g2 = jnp.where(inside, h2, 0.0), jnp.where(inside, g2, 0.0)
        half_inv = STEP * inv_volume[:, here]
        src = source[pl.ds(pl.multiple_of(i * LAYERS, LAYERS), LAYERS), :]
        onward = []
        for s in range(2):
            y = species[s, :, here]
            top = ghosts[3 + s : 4 + s, here]
            last = y[LAYERS - 1 :]
            y0 = below_of(y, ghosts[s : s + 1, here])
            y1 = before_of(y, species[s, :, back])
            y2 = pltpu.roll(y, 1, 1)
            f0 = h0 * (y + y0) - (g0 * d[s]) * (y - y0)
            ft = ht * (top + last) - (gt * d[s]) * (top - last)
            f1 = h1 * (y + y1) - (g1 * d[s]) * (y - y1)
            f2 = h2 * (y + y2) - (g2 * d[s]) * (y - y2)
            u0 = jnp.where(layer == LAYERS - 1, ft, pltpu.roll(f0, LAYERS - 1, 0))
            u1 = pltpu.roll(jnp.where(right_half, f1, carry[s]), 64, 1)
            u2 = pltpu.roll(f2, 127, 1)
            divergence = (u0 - f0) + ((u1 - f1) + (u2 - f2))
            delta = fuel if s == 0 else 0.0
            out[s, :, here] = y + half_inv * (src * (delta - y) - divergence)
            onward.append(f1)
        return tuple(onward)

    carry = (jnp.zeros((LAYERS, 128), F32),) * 2
    writes = []
    for g in range(4):
        carry = lax.fori_loop(g * 8, g * 8 + 8, strip, carry, unroll=4)
        done = pl.ds((3 - g) * 1024, 1024)
        writes.append(pltpu.make_async_copy(out.at[:, :, done], new_species.at[:, :, done], out_sems.at[g]))
        writes[-1].start()
    for write in writes:
        write.wait()


def spec(space=pltpu.VMEM):
    return pl.BlockSpec(memory_space=space)


HBM = pl.BlockSpec(memory_space=pltpu.HBM)


def params(**kw):
    return pltpu.CompilerParams(vmem_limit_bytes=VMEM_LIMIT, **kw)


def shape(*dims):
    return jax.ShapeDtypeStruct(dims, F32)


def body(
    species, interface_normal_flow, face_diffusion, inv_volume, diffusivity, low_partner, high_partner,
    low_orient, high_orient, droplet_table, parcel_block, parcel_cell, parcel_live,
):
    pick, oriented, unoriented, spread = constants()
    dma = pltpu.SemaphoreType.DMA
    vm = lambda *dims: pltpu.VMEM(dims, F32)
    iv = lambda *dims: pltpu.VMEM(dims, jnp.int32)
    bv = lambda *dims: pltpu.VMEM(dims, BF16)
    z_sum, source, ghosts, parcels, change = pl.pallas_call(
        exchange_kernel,
        out_shape=(shape(NQ, 8, JK), shape(1024, 128), shape(8, JK), shape(NB, ROWS, 128), shape(NB * CAP, 128)),
        in_specs=[HBM] * 16,
        out_specs=(spec(),) * 5,
        scratch_shapes=[
            pltpu.SMEM((2,), F32), vm(2, LAYERS, JK), vm(3, LAYERS, JK), vm(8, JK), *[iv(1, 64)] * 4, vm(256, 128), *[iv(1, 256)] * 3,
            bv(512, 64), bv(64, 1024), bv(64, 1024), bv(128, 1024),
            vm(NB, ROWS, 128), vm(NB, ROWS, 128), vm(NB, ROWS, 128), vm(NQ, NB, ROWS, 128),
            vm(NQ, 8, JK), vm(3, 8, JK), vm(8, JK), vm(8, 256), vm(8, 256), bv(1024, 1536),
            dma((16,)), dma((2 * CHUNKS + 1, 3)), dma((2 * CHUNKS + 1, 3)), dma((2,)), dma((2,)), dma((4,)), dma((3,)), dma,
        ],
        compiler_params=params(collective_id=0, has_side_effects=True),
        name="exchange",
    )(*(pltpu.with_memory_space_constraint(x, pltpu.HBM) for x in (
        diffusivity, species, interface_normal_flow, face_diffusion, low_partner, high_partner, low_orient, high_orient,
        droplet_table, parcel_block.reshape(1, -1), parcel_cell.reshape(1, -1), parcel_live.reshape(1, -1),
        pick, oriented, unoriented, spread,
    )))
    new_species, arrived = pl.pallas_call(
        final_kernel,
        out_shape=(shape(2, LAYERS, JK), shape(384, 128)),
        in_specs=[pl.BlockSpec(memory_space=pltpu.SMEM)] + [spec()] * 9,
        out_specs=(HBM, spec()),
        scratch_shapes=[vm(2, LAYERS, JK), dma((4,))],
        compiler_params=params(),
        name="final",
    )(
        diffusivity, species, interface_normal_flow, face_diffusion, inv_volume, z_sum.reshape(LAYERS, JK), source, ghosts,
        parcels.reshape(NB * ROWS, 128), change,
    )
    return new_species, arrived


def solution(mesh):
    placed = (
        P("sp", "blk", None), P(None, "blk", None), P(None, "blk", None), P("blk", None), P("sp"),
        P("blk", None), P("blk", None), P("blk", None), P("blk", None),
        P(("blk", "sp"), None), P(("blk", "sp"), None), P(("blk", "sp")), P(("blk", "sp")),
    )
    return jax.shard_map(
        body, mesh=mesh, in_specs=placed, out_specs=(P("sp", "blk", None), P(("blk", "sp"), None)), check_vma=False,
    )
```

```python
import functools
import jax
import jax.numpy as jnp
import numpy as np
from jax import lax
from jax.experimental import pallas as pl
from jax.experimental.pallas import tpu as pltpu
from jax.sharding import PartitionSpec as P

NB = 64
NQ = 4
CAP = 6
ROWS = 8
CHUNKS = 2
NY = 4
NW = 16
LAYERS = 32
JK = 4096
MESH = pl.DeviceIdType.MESH
F32 = jnp.float32
BF16 = jnp.bfloat16
STEP = 0.5
DRAG = 0.3
VMEM_LIMIT = 36 * 1024 * 1024


def constants():
    lane = np.arange(512)
    cell = np.arange(64)
    pick = (lane[:, None] // 64 == cell[None, :] // 8) & (lane[:, None] % 8 == cell[None, :] % 8)
    r, c = cell // 8, cell % 8
    oriented, unoriented = [], []
    for code in range(8):
        f_row = (lambda v: 7 - v) if code & 1 else (lambda v: v)
        f_col = (lambda v: 7 - v) if code & 2 else (lambda v: v)
        r2, c2 = f_row(r), f_col(c)
        source = c2 * 8 + r2 if code & 4 else r2 * 8 + c2
        oriented += [cell[:, None] == source[None, :]] * 2
        source = f_row(c) * 8 + f_col(r) if code & 4 else f_row(r) * 8 + f_col(c)
        unoriented += [cell[:, None] == source[None, :]] * 2
    spread = np.zeros((128, 1024), bool)
    spread[:64, :512] = pick.T
    spread[64:, 512:] = pick.T
    pick3 = np.zeros((1536, 192), bool)
    for k in range(3):
        pick3[k * 512 : (k + 1) * 512, k * 64 : (k + 1) * 64] = pick
    thrice = lambda m: np.concatenate([m] * 3, 0)
    asb = lambda m: jnp.asarray(m.astype(np.float32), BF16)
    return asb(pick3), asb(thrice(np.concatenate(oriented, 1))), asb(thrice(np.concatenate(unoriented, 1))), asb(thrice(spread))


def pieces(x):
    hi = x.astype(BF16)
    rest = x - hi.astype(F32)
    mid = rest.astype(BF16)
    low = (rest - mid.astype(F32)).astype(BF16)
    return hi, mid, low


def mm(a, b):
    return lax.dot_general(a, b, (((1,), (0,)), ((), ())), preferred_element_type=F32)


def beside(x):
    return jnp.concatenate(pieces(x), axis=1)


def folded(x, n):
    return (x[:, :n] + x[:, n : 2 * n]) + x[:, 2 * n :]


def pick_rows(onehot, x):
    return folded(mm(onehot, beside(x)), x.shape[1])


def iota(shape, axis):
    return lax.broadcasted_iota(jnp.int32, shape, axis)


def ones(mask):
    return jnp.where(mask, 1.0, 0.0).astype(BF16)


def column(row):
    n = row.shape[1]
    return jnp.sum(jnp.where(iota((n, n), 0) == iota((n, n), 1), row, 0.0), axis=1, keepdims=True)


def strip_mask():
    lane = iota((8, 512), 1)
    return (lane % 64) // 8 == iota((8, 512), 0)


def stack_field(ref_slice):
    return jnp.concatenate([ref_slice[:, i * 128 : (i + 1) * 128] for i in range(LAYERS)], axis=0)


def lookups(cells, fields, ks):
    n = cells.shape[0]
    whole = cells.astype(jnp.int32)
    row = ((whole & 4095) >> 7) * LAYERS + (whole >> 12)
    hot = ones(iota((n, 1024), 1) == row)
    here = iota((n, 128), 1) == (whole & 127)
    for k in ks:
        yield jnp.sum(jnp.where(here, folded(mm(hot, fields[k]), 128), 0.0), axis=1, keepdims=True)


def ranks(block, live):
    n = block.shape[1]
    alive = live[...] == 1
    target = block[...].astype(F32)
    key = jnp.where(alive, target, -1.0)
    key_col = column(key)
    same = key_col == key
    first, second = iota((n, n), 0), iota((n, n), 1)
    rank = jnp.sum(jnp.where(same & (first < second), 1.0, 0.0), axis=0, keepdims=True)
    rank_col = jnp.sum(jnp.where(same & (second < first), 1.0, 0.0), axis=1, keepdims=True)
    return jnp.where(alive, target * ROWS, -1.0), jnp.where(alive, target * ROWS + rank, -1.0), rank_col


def meta_rows(table, cell, rank_col):
    rows = table[...]
    lane = iota(rows.shape, 1)
    cell_col = column(cell[...].astype(F32))
    boil = jnp.maximum(rows, 0.0) + jnp.log1p(jnp.exp(-jnp.abs(rows)))
    sig = 1.0 / (1.0 + jnp.exp(-rows))
    kind = lane & 7
    meta = jnp.where(kind == 0, cell_col, jnp.where(kind == 1, boil[:, 1:2], jnp.where(kind == 2, sig[:, 2:3], jnp.where(kind == 3, 1.0, 0.0))))
    return jnp.where((lane >> 3).astype(F32) == rank_col, meta, 0.0)


def turned_tiles(faces, pick, oriented, unoriented, high_code, low_code):
    mask = strip_mask()
    strips = []
    for face in faces:
        for jt in range(8):
            strips.append(jnp.where(mask, face[:, jt * 512 : (jt + 1) * 512], 0.0))
    tiles = mm(beside(jnp.concatenate(strips, axis=0)), pick[...]).astype(BF16)
    turned = mm(tiles[:128], oriented[...])
    unturned = mm(tiles[128:], unoriented[...])

    def choose(x, code):
        out = x[:, :128]
        for o in range(1, 8):
            out = jnp.where(code == o, x[:, o * 128 : (o + 1) * 128], out)
        return out

    return [choose(turned[k * 64 : (k + 1) * 64], high_code) for k in range(2)] + [
        choose(unturned[k * 64 : (k + 1) * 64], low_code) for k in range(4)
    ]


def addressed(keys, values, out):
    keys, values = jnp.concatenate(keys, axis=1), jnp.concatenate(values, axis=0)
    out[...] = pick_rows(ones(iota((NB * ROWS, keys.shape[1]), 0).astype(F32) == keys), values)


def exchange_kernel(
    dif_in, species_in, flow_in, diffusion_in, lp_in, hp_in, lo_in, ho_in, table_in, block_in, cell_in, live_in,
    pick_in, oriented_in, unoriented_in, spread_in,
    z_sum, source, ghosts, parcels, change,
    dif, species, flow, edge, lp, hp, lo, ho, table, block, cell, live, pick, oriented, unoriented, spread,
    msg_a, msg_b, mid_a, mid_b, recv_a, forward, z_part, z_got, z_mine, fuel, fuel_col, fields, hot,
    load_sems, sems, recv_sems, near_send, near_recv, wide_send, wide_recv, local_sems, fuel_send, fuel_recv,
):
    b, q = lax.axis_index("blk"), lax.axis_index("sp")
    y, w = lax.div(b, NW), lax.rem(b, NW)
    pairs = (
        (species_in, species), (dif_in, dif), (flow_in.at[0, pl.ds(0, 8)], edge.at[0]), (diffusion_in.at[0, pl.ds(0, 8)], edge.at[1]),
        (table_in, table), (block_in, block), (live_in, live), (cell_in, cell), (lp_in, lp), (hp_in, hp), (lo_in, lo), (ho_in, ho),
        (pick_in, pick), (oriented_in, oriented), (unoriented_in, unoriented), (flow_in, flow), (spread_in, spread),
    )
    loads = [pltpu.make_async_copy(src, dst, load_sems.at[k]) for k, (src, dst) in enumerate(pairs)]
    for load in loads:
        load.start()
    barrier = pltpu.get_barrier_semaphore()

    for d in range(1, NQ):
        pl.semaphore_signal(barrier, inc=1, device_id=(b, lax.rem(q + d, NQ)), device_id_type=MESH)
    for d in range(1, NY):
        pl.semaphore_signal(barrier, inc=1, device_id=(lax.rem(y + d, NY) * NW + w, q), device_id_type=MESH)
    for d in range(1, NW):
        pl.semaphore_signal(barrier, inc=1, device_id=(y * NW + lax.rem(w + d, NW), q), device_id_type=MESH)
    for load in loads[:15]:
        load.wait()

    d0, d1 = dif[0], dif[1]
    for k in range(NQ):
        z_part[k] = d0 * species[0, k * 8 : (k + 1) * 8] + d1 * species[1, k * 8 : (k + 1) * 8]
    to_block, to_slot, rank_col = ranks(block, live)
    up0, up1, lo0, lo1, fl, df = turned_tiles(
        [
            species[0, LAYERS - 1 : LAYERS, :], species[1, LAYERS - 1 : LAYERS, :], species[0, 0:1, :], species[1, 0:1, :],
            edge[0, 0:1, :], edge[1, 0:1, :],
        ],
        pick, oriented, unoriented, column(ho[...].astype(F32)), column(lo[...].astype(F32)),
    )
    left = iota((NB, 128), 1) < 64
    high, low = hp[...].astype(F32) * ROWS, lp[...].astype(F32) * ROWS
    addressed(
        [to_block, high + 1.0, low + 1.0, low + 2.0],
        [
            meta_rows(table, cell, rank_col), jnp.where(left, d0 * up0 + d1 * up1, 0.0), jnp.where(left, 0.0, d0 * lo0 + d1 * lo1),
            jnp.where(left, fl, df),
        ],
        msg_a.reshape(NB * ROWS, 128),
    )
    pl.semaphore_wait(barrier, NQ + NY + NW - 3)

    def sp_copy(src, dst, k, d):
        return pltpu.make_async_remote_copy(
            src_ref=src, dst_ref=dst, send_sem=sems.at[k, d - 1], recv_sem=recv_sems.at[k, d - 1],
            device_id=(b, lax.rem(q + d, NQ)), device_id_type=MESH,
        )

    wide = JK // CHUNKS
    part = [pl.ds(c * wide, wide) for c in range(CHUNKS)]
    scatter = [
        [sp_copy(z_part.at[lax.rem(q + d, NQ), :, part[c]], z_got.at[d - 1, :, part[c]], c, d) for d in (2, 1, 3)]
        for c in range(CHUNKS)
    ]
    gather = [
        [sp_copy(z_mine.at[:, part[c]], z_sum.at[q, :, part[c]], CHUNKS + c, d) for d in (2, 1, 3)] for c in range(CHUNKS)
    ]

    rows_a, rows_b = pl.ds(0, 3), pl.ds(0, ROWS)

    def along_y(msg, mid, rows, k):
        copies = []
        for d in (2, 1, 3):
            to = lax.rem(y + d, NY)
            copies.append(
                pltpu.make_async_remote_copy(
                    src_ref=msg.at[pl.ds(to * NW, NW), rows], dst_ref=mid.at[y, :, rows],
                    send_sem=near_send.at[k, d - 1], recv_sem=near_recv.at[k, d - 1],
                    device_id=(to * NW + w, q), device_id_type=MESH,
                )
            )
        keep = pltpu.make_async_copy(msg.at[pl.ds(y * NW, NW), rows], mid.at[y, :, rows], local_sems.at[2 * k])
        return copies, keep

    def across(mid, recv, rows, k):
        def step(d, carry):
            to = lax.rem(w + 1 + lax.rem(d + 7, NW - 1), NW)
            pltpu.make_async_remote_copy(
                src_ref=mid.at[:, to, rows], dst_ref=recv.at[:, w, rows], send_sem=wide_send.at[k], recv_sem=wide_recv.at[k],
                device_id=(y * NW + to, q), device_id_type=MESH,
            ).start()
            return carry

        lax.fori_loop(0, NW - 1, step, 0)
        keep = pltpu.make_async_copy(mid.at[:, w, rows], recv.at[:, w, rows], local_sems.at[2 * k + 1])
        keep.start()
        return keep

    most = pl.ds(0, NW - 1)
    first_a, keep_a = along_y(msg_a, mid_a, rows_a, 0)
    keep_a.start()
    for copy in first_a:
        copy.start()
    for copies in scatter:
        for copy in copies:
            copy.start()

    loads[15].wait()
    loads[16].wait()

    def cut(i, carry):
        here = pl.ds(pl.multiple_of(i * 128, 128), 128)
        there = pl.ds(pl.multiple_of(i * LAYERS, LAYERS), LAYERS)
        fields[0, there, :] = beside(species[0, :, here])
        for k in range(3):
            fields[k + 1, there, :] = beside(flow[k, :, here])
        return carry

    lax.fori_loop(0, LAYERS // 2, cut, 0, unroll=2)
    keep_a.wait()
    for copy in first_a:
        copy.wait_recv()
    keep_a = across(mid_a, recv_a, rows_a, 0)
    lax.fori_loop(LAYERS // 2, LAYERS, cut, 0, unroll=2)
    addressed(
        [to_slot, high + 6.0, low + 7.0],
        [table[...], jnp.where(left, up0, up1), jnp.where(left, lo0, lo1)],
        msg_b.reshape(NB * ROWS, 128),
    )
    first_b, keep_b = along_y(msg_b, mid_b, rows_b, 1)
    keep_b.start()
    for copy in first_b:
        copy.start()

    def gather_part(c):
        for copy in scatter[c]:
            copy.wait_recv()
        total = (z_part[q, :, part[c]] + z_got[0, :, part[c]]) + (z_got[1, :, part[c]] + z_got[2, :, part[c]])
        z_mine[:, part[c]] = total
        for copy in gather[c]:
            copy.start()
        z_sum[q, :, part[c]] = total

    keep_a.wait()
    pltpu.make_async_copy(recv_a.at[:, most, rows_a], recv_a.at[:, most, rows_a], wide_recv.at[0]).wait()
    two = pl.ds(0, 2)
    onward = [sp_copy(recv_a.at[:, :, two], forward.at[q, :, :, two], 2 * CHUNKS, d) for d in (2, 1, 3)]
    for copy in onward:
        copy.start()
    keep_f = pltpu.make_async_copy(recv_a.at[:, :, two], forward.at[q, :, :, two], local_sems.at[4])
    keep_f.start()
    gather_part(0)

    keep_b.wait()
    for copy in first_b:
        copy.wait_recv()
    keep_b = across(mid_b, parcels, rows_b, 1)

    got = recv_a.reshape(NB * ROWS, 128)
    got_b = parcels.reshape(NB * ROWS, 128)
    seen = forward.reshape(NQ * NB * ROWS, 128)
    own = got[pl.ds(0, NB, stride=ROWS), :]
    own_cells = jnp.concatenate([own[:, 8 * r : 8 * r + 1] for r in range(CAP)], axis=0)
    speeds = list(lookups(own_cells, fields, (1, 2, 3)))

    @pl.when(q != 0)
    def _():
        for c in range(1, CHUNKS):
            gather_part(c)

    keep_f.wait()
    for copy in onward:
        copy.wait_recv()
    meta = seen[pl.ds(0, NB * NQ, stride=ROWS), :]
    shared = [
        pltpu.make_async_remote_copy(
            src_ref=fuel, dst_ref=fuel, send_sem=fuel_send.at[d - 1], recv_sem=fuel_recv, device_id=(b, d), device_id_type=MESH
        )
        for d in (2, 1, 3)
    ]

    @pl.when(q == 0)
    def _():
        lane = iota((NB * NQ, 128), 1)
        found = jnp.zeros((NB * NQ, 128), F32)
        cells = jnp.concatenate([meta[:, 8 * r : 8 * r + 1] for r in range(CAP)], axis=0)
        [value] = lookups(cells, fields, (0,))
        for r in range(CAP):
            found = jnp.where(lane == r, value[r * NB * NQ : (r + 1) * NB * NQ], found)
        fuel[...] = jnp.transpose(found)[:8]
        for copy in shared:
            copy.start()
        for c in range(1, CHUNKS):
            gather_part(c)

    meta_t = jnp.transpose(meta)
    cells = jnp.concatenate([meta_t[8 * r : 8 * r + 1, :] for r in range(CAP)], axis=1).astype(jnp.int32)
    row = ((cells & 4095) >> 7) * LAYERS + (cells >> 12)
    for m in range(4):
        hot[m * 256 : (m + 1) * 256, :] = ones(iota((256, NB * NQ * CAP), 0) + m * 256 == row)

    def fill_ghosts():
        keep_b.wait()
        pltpu.make_async_copy(parcels.at[:, most], parcels.at[:, most], wide_recv.at[1]).wait()
        low_sel = ones(iota((NB, NB), 1).astype(F32) == column(lp[...].astype(F32)))
        high_sel = ones(iota((NB, NB), 1).astype(F32) == column(hp[...].astype(F32)))
        z_tiles = seen[pl.ds(1, NB * NQ, stride=ROWS), :]
        z_tiles = (z_tiles[:64] + z_tiles[64:128]) + (z_tiles[128:192] + z_tiles[192:])
        below = pick_rows(low_sel, jnp.concatenate([got_b[pl.ds(6, NB, stride=ROWS), :], z_tiles], axis=1))
        above = pick_rows(
            high_sel, jnp.concatenate([got_b[pl.ds(7, NB, stride=ROWS), :], got[pl.ds(2, NB, stride=ROWS), :], z_tiles], axis=1)
        )
        tiles = jnp.concatenate([below[:, :128], above[:, :128], above[:, 128:256], jnp.where(left, below[:, 128:], above[:, 256:])], axis=0)
        spread_tiles = mm(beside(tiles), spread[...])
        mask = strip_mask()
        slots = ((0, 1), (3, 4), (6, 7), (2, 5))
        for g in range(4):
            for jt in range(8):
                strip = spread_tiles[g * 64 + jt * 8 : g * 64 + jt * 8 + 8]
                for side in range(2):
                    value = jnp.sum(jnp.where(mask, strip[:, side * 512 : (side + 1) * 512], 0.0), axis=0, keepdims=True)
                    ghosts[slots[g][side] : slots[g][side] + 1, jt * 512 : (jt + 1) * 512] = value

    fill_ghosts()

    @pl.when(q != 0)
    def _():
        shared[0].wait_recv()

    found_col = jnp.transpose(jnp.concatenate([fuel[...], jnp.zeros((120, NB * NQ), F32)], axis=0))
    fuel_col[...] = found_col
    lane = iota((NB * NQ, 128), 1)
    mass = []
    for r in range(CAP):
        k = 8 * r
        gone = meta[:, k + 1 : k + 2] * (meta[:, k + 2 : k + 3] - found_col[:, r : r + 1])
        at = meta[:, k : k + 1].astype(jnp.int32) & 127
        mass.append(beside(jnp.where(lane == at, gone, 0.0)))
    source[...] = folded(mm(hot[...], jnp.concatenate(mass, axis=0)), 128)

    own_fuel = fuel_col[pl.ds(pl.multiple_of(q * NB, NB), NB), :]
    lane = iota((NB, 128), 1)
    for r in range(CAP):
        k = 8 * r
        gone = own[:, k + 1 : k + 2] * (own[:, k + 2 : k + 3] - own_fuel[:, r : r + 1])
        drag = DRAG * own[:, k + 3 : k + 4]
        moved = jnp.where(lane == 0, -gone, 0.0)
        for c in range(3):
            moved = jnp.where(lane == 3 + c, drag * speeds[c][r * NB : (r + 1) * NB], moved)
        change[pl.ds(r, NB, stride=CAP), :] = moved

    @pl.when(q == 0)
    def _():
        for copy in shared:
            copy.wait_send()

    pltpu.make_async_copy(mid_a.at[:, most, rows_a], mid_a.at[:, most, rows_a], wide_send.at[0]).wait()
    pltpu.make_async_copy(mid_b.at[:, most], mid_b.at[:, most], wide_send.at[1]).wait()
    for copy in first_a + first_b:
        copy.wait_send()
    for copies in scatter:
        for copy in copies:
            copy.wait_send()
    for copy in onward:
        copy.wait_send()
    for copies in gather:
        for copy in copies:
            copy.wait()


def final_kernel(
    dif, species, flow, diffusion, inv_volume, z_sum, source, ghosts, parcels, change, new_species, arrived, out, out_sems,
):
    q = lax.axis_index("sp")
    d = (dif[0], dif[1])
    lane = iota((NB, 128), 1)
    keep = jnp.where((lane >= 3) & (lane <= 5), 1.0 - DRAG, 1.0)
    for r in range(CAP):
        arrived[pl.ds(r, NB, stride=CAP), :] = parcels[pl.ds(r, NB, stride=ROWS), :] * keep + change[pl.ds(r, NB, stride=CAP), :]

    lane = iota((LAYERS, 128), 1)
    layer = iota((LAYERS, 128), 0)
    fuel = jnp.where(q == 0, 1.0, 0.0)
    right_half = lane >= 64
    inside = (lane & 63) != 0

    def strip(n, carry):
        i = LAYERS - 1 - n
        here = pl.ds(pl.multiple_of(i * 128, 128), 128)
        back = pl.ds(pl.multiple_of(jnp.maximum(i - 1, 0) * 128, 128), 128)
        beyond_wall = (i > 0) | right_half

        def below_of(x, ghost):
            return jnp.where(layer == 0, ghost, pltpu.roll(x, 1, 0))

        def before_of(x, previous):
            return pltpu.roll(jnp.where(right_half, previous, x), 64, 1)

        z = z_sum[:, here]
        g0, g1, g2 = diffusion[0, :, here], diffusion[1, :, here], diffusion[2, :, here]
        gt = ghosts[7:8, here]
        h0 = 0.5 * (flow[0, :, here] + g0 * (z - below_of(z, ghosts[2:3, here])))
        ht = 0.5 * (ghosts[6:7, here] + gt * (ghosts[5:6, here] - z[LAYERS - 1 :]))
        h1 = 0.5 * (flow[1, :, here] + g1 * (z - before_of(z, z_sum[:, back])))
        h2 = 0.5 * (flow[2, :, here] + g2 * (z - pltpu.roll(z, 1, 1)))
        h1, g1 = jnp.where(beyond_wall, h1, 0.0), jnp.where(beyond_wall, g1, 0.0)
        h2, g2 = jnp.where(inside, h2, 0.0), jnp.where(inside, g2, 0.0)
        half_inv = STEP * inv_volume[:, here]
        src = source[pl.ds(pl.multiple_of(i * LAYERS, LAYERS), LAYERS), :]
        onward = []
        for s in range(2):
            y = species[s, :, here]
            top = ghosts[3 + s : 4 + s, here]
            last = y[LAYERS - 1 :]
            y0 = below_of(y, ghosts[s : s + 1, here])
            y1 = before_of(y, species[s, :, back])
            y2 = pltpu.roll(y, 1, 1)
            f0 = h0 * (y + y0) - (g0 * d[s]) * (y - y0)
            ft = ht * (top + last) - (gt * d[s]) * (top - last)
            f1 = h1 * (y + y1) - (g1 * d[s]) * (y - y1)
            f2 = h2 * (y + y2) - (g2 * d[s]) * (y - y2)
            u0 = jnp.where(layer == LAYERS - 1, ft, pltpu.roll(f0, LAYERS - 1, 0))
            u1 = pltpu.roll(jnp.where(right_half, f1, carry[s]), 64, 1)
            u2 = pltpu.roll(f2, 127, 1)
            divergence = (u0 - f0) + ((u1 - f1) + (u2 - f2))
            delta = fuel if s == 0 else 0.0
            out[s, :, here] = y + half_inv * (src * (delta - y) - divergence)
            onward.append(f1)
        return tuple(onward)

    carry = (jnp.zeros((LAYERS, 128), F32),) * 2
    writes = []
    for g in range(4):
        carry = lax.fori_loop(g * 8, g * 8 + 8, strip, carry, unroll=4)
        done = pl.ds((3 - g) * 1024, 1024)
        writes.append(pltpu.make_async_copy(out.at[:, :, done], new_species.at[:, :, done], out_sems.at[g]))
        writes[-1].start()
    for write in writes:
        write.wait()


def spec(space=pltpu.VMEM):
    return pl.BlockSpec(memory_space=space)


HBM = pl.BlockSpec(memory_space=pltpu.HBM)


def params(**kw):
    return pltpu.CompilerParams(vmem_limit_bytes=VMEM_LIMIT, **kw)


def shape(*dims):
    return jax.ShapeDtypeStruct(dims, F32)


def body(
    species, interface_normal_flow, face_diffusion, inv_volume, diffusivity, low_partner, high_partner,
    low_orient, high_orient, droplet_table, parcel_block, parcel_cell, parcel_live,
):
    pick, oriented, unoriented, spread = constants()
    dma = pltpu.SemaphoreType.DMA
    vm = lambda *dims: pltpu.VMEM(dims, F32)
    iv = lambda *dims: pltpu.VMEM(dims, jnp.int32)
    bv = lambda *dims: pltpu.VMEM(dims, BF16)
    z_sum, source, ghosts, parcels, change = pl.pallas_call(
        exchange_kernel,
        out_shape=(shape(NQ, 8, JK), shape(1024, 128), shape(8, JK), shape(NY, NW, ROWS, 128), shape(NB * CAP, 128)),
        in_specs=[HBM] * 16,
        out_specs=(spec(),) * 5,
        scratch_shapes=[
            pltpu.SMEM((2,), F32), vm(2, LAYERS, JK), vm(3, LAYERS, JK), vm(2, 8, JK), *[iv(1, 64)] * 4, vm(256, 128), *[iv(1, 256)] * 3,
            bv(1536, 192), bv(192, 1024), bv(192, 1024), bv(384, 1024),
            vm(NB, ROWS, 128), vm(NB, ROWS, 128), *[vm(NY, NW, ROWS, 128)] * 3, vm(NQ, NY, NW, ROWS, 128),
            vm(NQ, 8, JK), vm(3, 8, JK), vm(8, JK), vm(8, 256), vm(256, 128), bv(4, 1024, 384), bv(1024, 1536),
            dma((17,)), dma((2 * CHUNKS + 1, 3)), dma((2 * CHUNKS + 1, 3)), dma((2, 3)), dma((2, 3)), dma((2,)), dma((2,)), dma((5,)), dma((3,)), dma,
        ],
        compiler_params=params(collective_id=0, has_side_effects=True),
        name="exchange",
    )(*(pltpu.with_memory_space_constraint(x, pltpu.HBM) for x in (
        diffusivity, species, interface_normal_flow, face_diffusion, low_partner, high_partner, low_orient, high_orient,
        droplet_table, parcel_block.reshape(1, -1), parcel_cell.reshape(1, -1), parcel_live.reshape(1, -1),
        pick, oriented, unoriented, spread,
    )))
    new_species, arrived = pl.pallas_call(
        final_kernel,
        out_shape=(shape(2, LAYERS, JK), shape(384, 128)),
        in_specs=[pl.BlockSpec(memory_space=pltpu.SMEM)] + [spec()] * 9,
        out_specs=(HBM, spec()),
        scratch_shapes=[vm(2, LAYERS, JK), dma((4,))],
        compiler_params=params(),
        name="final",
    )(
        diffusivity, species, interface_normal_flow, face_diffusion, inv_volume, z_sum.reshape(LAYERS, JK), source, ghosts,
        parcels.reshape(NB * ROWS, 128), change,
    )
    return new_species, arrived


def solution(mesh):
    placed = (
        P("sp", "blk", None), P(None, "blk", None), P(None, "blk", None), P("blk", None), P("sp"),
        P("blk", None), P("blk", None), P("blk", None), P("blk", None),
        P(("blk", "sp"), None), P(("blk", "sp"), None), P(("blk", "sp")), P(("blk", "sp")),
    )
    return jax.shard_map(
        body, mesh=mesh, in_specs=placed, out_specs=(P("sp", "blk", None), P(("blk", "sp"), None)), check_vma=False,
    )
```

```python
import functools
import jax
import jax.numpy as jnp
import numpy as np
from jax import lax
from jax.experimental import pallas as pl
from jax.experimental.pallas import tpu as pltpu
from jax.sharding import PartitionSpec as P

NB = 64
NQ = 4
CAP = 6
ROWS = 8
CHUNKS = 2
NY = 4
NW = 16
CUT = 16
KINDS = 3
LAYERS = 32
JK = 4096
MESH = pl.DeviceIdType.MESH
F32 = jnp.float32
BF16 = jnp.bfloat16
STEP = 0.5
DRAG = 0.3
VMEM_LIMIT = 36 * 1024 * 1024


def constants():
    lane = np.arange(512)
    cell = np.arange(64)
    pick = (lane[:, None] // 64 == cell[None, :] // 8) & (lane[:, None] % 8 == cell[None, :] % 8)
    r, c = cell // 8, cell % 8
    oriented, unoriented = [], []
    for code in range(8):
        f_row = (lambda v: 7 - v) if code & 1 else (lambda v: v)
        f_col = (lambda v: 7 - v) if code & 2 else (lambda v: v)
        r2, c2 = f_row(r), f_col(c)
        source = c2 * 8 + r2 if code & 4 else r2 * 8 + c2
        oriented += [cell[:, None] == source[None, :]] * 2
        source = f_row(c) * 8 + f_col(r) if code & 4 else f_row(r) * 8 + f_col(c)
        unoriented += [cell[:, None] == source[None, :]] * 2
    spread = np.zeros((128, 1024), bool)
    spread[:64, :512] = pick.T
    spread[64:, 512:] = pick.T
    pick3 = np.zeros((1536, 192), bool)
    for k in range(3):
        pick3[k * 512 : (k + 1) * 512, k * 64 : (k + 1) * 64] = pick
    thrice = lambda m: np.concatenate([m] * 3, 0)
    asb = lambda m: jnp.asarray(m.astype(np.float32), BF16)
    return asb(pick3), asb(thrice(np.concatenate(oriented, 1))), asb(thrice(np.concatenate(unoriented, 1))), asb(thrice(spread))


def pieces(x):
    hi = x.astype(BF16)
    rest = x - hi.astype(F32)
    mid = rest.astype(BF16)
    low = (rest - mid.astype(F32)).astype(BF16)
    return hi, mid, low


def mm(a, b):
    return lax.dot_general(a, b, (((1,), (0,)), ((), ())), preferred_element_type=F32)


def beside(x):
    return jnp.concatenate(pieces(x), axis=1)


def folded(x, n):
    return (x[:, :n] + x[:, n : 2 * n]) + x[:, 2 * n :]


def pick_rows(onehot, x):
    return folded(mm(onehot, beside(x)), x.shape[1])


def iota(shape, axis):
    return lax.broadcasted_iota(jnp.int32, shape, axis)


def ones(mask):
    return jnp.where(mask, 1.0, 0.0).astype(BF16)


def column(row):
    n = row.shape[1]
    return jnp.sum(jnp.where(iota((n, n), 0) == iota((n, n), 1), row, 0.0), axis=1, keepdims=True)


def strip_mask():
    lane = iota((8, 512), 1)
    return (lane % 64) // 8 == iota((8, 512), 0)


def stack_field(ref_slice):
    return jnp.concatenate([ref_slice[:, i * 128 : (i + 1) * 128] for i in range(LAYERS)], axis=0)


def lookups(cells, fields, ks):
    n = cells.shape[0]
    whole = cells.astype(jnp.int32)
    row = ((whole & 4095) >> 7) * LAYERS + (whole >> 12)
    hot = ones(iota((n, 1024), 1) == row)
    here = iota((n, 128), 1) == (whole & 127)
    for k in ks:
        yield jnp.sum(jnp.where(here, folded(mm(hot, fields[k]), 128), 0.0), axis=1, keepdims=True)


def ranks(block, live):
    n = block.shape[1]
    alive = live[...] == 1
    target = block[...].astype(F32)
    key = jnp.where(alive, target, -1.0)
    key_col = column(key)
    same = key_col == key
    first, second = iota((n, n), 0), iota((n, n), 1)
    rank = jnp.sum(jnp.where(same & (first < second), 1.0, 0.0), axis=0, keepdims=True)
    rank_col = jnp.sum(jnp.where(same & (second < first), 1.0, 0.0), axis=1, keepdims=True)
    return jnp.where(alive, target * ROWS, -1.0), jnp.where(alive, target * ROWS + rank, -1.0), rank_col


def meta_rows(table, cell, rank_col):
    rows = table[...]
    lane = iota(rows.shape, 1)
    cell_col = column(cell[...].astype(F32))
    boil = jnp.maximum(rows, 0.0) + jnp.log1p(jnp.exp(-jnp.abs(rows)))
    sig = 1.0 / (1.0 + jnp.exp(-rows))
    kind = lane & 7
    meta = jnp.where(kind == 0, cell_col, jnp.where(kind == 1, boil[:, 1:2], jnp.where(kind == 2, sig[:, 2:3], jnp.where(kind == 3, 1.0, 0.0))))
    return jnp.where((lane >> 3).astype(F32) == rank_col, meta, 0.0)


def turned_tiles(faces, pick, oriented, unoriented, high_code, low_code):
    mask = strip_mask()
    strips = []
    for face in faces:
        for jt in range(8):
            strips.append(jnp.where(mask, face[:, jt * 512 : (jt + 1) * 512], 0.0))
    tiles = mm(beside(jnp.concatenate(strips, axis=0)), pick[...]).astype(BF16)
    turned = mm(tiles[:128], oriented[...])
    unturned = mm(tiles[128:], unoriented[...])

    def choose(x, code):
        out = x[:, :128]
        for o in range(1, 8):
            out = jnp.where(code == o, x[:, o * 128 : (o + 1) * 128], out)
        return out

    return [choose(turned[k * 64 : (k + 1) * 64], high_code) for k in range(2)] + [
        choose(unturned[k * 64 : (k + 1) * 64], low_code) for k in range(4)
    ]


def addressed(keys, values, out):
    keys, values = jnp.concatenate(keys, axis=1), jnp.concatenate(values, axis=0)
    out[...] = pick_rows(ones(iota((NB * ROWS, keys.shape[1]), 0).astype(F32) == keys), values)


def exchange_kernel(
    dif_in, species_in, flow_in, diffusion_in, lp_in, hp_in, lo_in, ho_in, table_in, block_in, cell_in, live_in,
    pick_in, oriented_in, unoriented_in, spread_in,
    z_sum, source, ghosts, parcels, change,
    dif, species, flow, edge, lp, hp, lo, ho, table, block, cell, live, pick, oriented, unoriented, spread,
    msg_a, msg_b, mid_a, mid_b, pack_a, recv_a, forward, z_part, z_got, z_mine, fuel, fuel_col, fields, hot,
    load_sems, sems, recv_sems, near_send, near_recv, wide_send, wide_recv, local_sems, fuel_send, fuel_recv,
):
    b, q = lax.axis_index("blk"), lax.axis_index("sp")
    y, w = lax.div(b, NW), lax.rem(b, NW)
    pairs = (
        (species_in, species), (dif_in, dif), (flow_in.at[0, pl.ds(0, 8)], edge.at[0]), (diffusion_in.at[0, pl.ds(0, 8)], edge.at[1]),
        (table_in, table), (block_in, block), (live_in, live), (cell_in, cell), (lp_in, lp), (hp_in, hp), (lo_in, lo), (ho_in, ho),
        (pick_in, pick), (oriented_in, oriented), (unoriented_in, unoriented), (flow_in, flow), (spread_in, spread),
    )
    loads = [pltpu.make_async_copy(src, dst, load_sems.at[k]) for k, (src, dst) in enumerate(pairs)]
    for load in loads:
        load.start()
    barrier = pltpu.get_barrier_semaphore()

    for d in range(1, NQ):
        pl.semaphore_signal(barrier, inc=1, device_id=(b, lax.rem(q + d, NQ)), device_id_type=MESH)
    for d in range(1, NY):
        pl.semaphore_signal(barrier, inc=1, device_id=(lax.rem(y + d, NY) * NW + w, q), device_id_type=MESH)
    for d in range(1, NW):
        pl.semaphore_signal(barrier, inc=1, device_id=(y * NW + lax.rem(w + d, NW), q), device_id_type=MESH)
    loads[0].wait()
    loads[1].wait()

    d0, d1 = dif[0], dif[1]
    for k in range(NQ):
        z_part[k] = d0 * species[0, k * 8 : (k + 1) * 8] + d1 * species[1, k * 8 : (k + 1) * 8]
    for load in loads[2:15]:
        load.wait()
    to_block, to_slot, rank_col = ranks(block, live)
    up0, up1, lo0, lo1, fl, df = turned_tiles(
        [
            species[0, LAYERS - 1 : LAYERS, :], species[1, LAYERS - 1 : LAYERS, :], species[0, 0:1, :], species[1, 0:1, :],
            edge[0, 0:1, :], edge[1, 0:1, :],
        ],
        pick, oriented, unoriented, column(ho[...].astype(F32)), column(lo[...].astype(F32)),
    )
    left = iota((NB, 128), 1) < 64
    high, low = hp[...].astype(F32) * ROWS, lp[...].astype(F32) * ROWS
    by_block = iota((NB, 256), 0).astype(F32) * ROWS == to_block
    tile_keys = jnp.concatenate([high, low], axis=1)
    by_tile = ones(iota((NB, 2 * NB), 0).astype(F32) * ROWS == tile_keys)
    z_tiles = jnp.concatenate([jnp.where(left, d0 * up0 + d1 * up1, 0.0), jnp.where(left, 0.0, d0 * lo0 + d1 * lo1)], axis=0)
    edges = jnp.concatenate([jnp.zeros((NB, 128), F32), jnp.where(left, fl, df)], axis=0)
    picked = pick_rows(by_tile, jnp.concatenate([z_tiles, edges], axis=1))
    kinds = (pick_rows(ones(by_block), meta_rows(table, cell, rank_col)), picked[:, :128], picked[:, 128:])
    for k in range(KINDS):
        for to in range(NY):
            msg_a[to, k] = kinds[k][to * NW : (to + 1) * NW]
    pl.semaphore_wait(barrier, NQ + NY + NW - 3)

    def sp_copy(src, dst, k, d):
        return pltpu.make_async_remote_copy(
            src_ref=src, dst_ref=dst, send_sem=sems.at[k, d - 1], recv_sem=recv_sems.at[k, d - 1],
            device_id=(b, lax.rem(q + d, NQ)), device_id_type=MESH,
        )

    wide = JK // CHUNKS
    part = [pl.ds(c * wide, wide) for c in range(CHUNKS)]
    scatter = [
        [sp_copy(z_part.at[lax.rem(q + d, NQ), :, part[c]], z_got.at[d - 1, :, part[c]], c, d) for d in (2, 1, 3)]
        for c in range(CHUNKS)
    ]
    gather = [
        [sp_copy(z_mine.at[:, part[c]], z_sum.at[q, :, part[c]], CHUNKS + c, d) for d in (2, 1, 3)] for c in range(CHUNKS)
    ]

    def along_y(msg, mid, k):
        copies = []
        for d in (2, 1, 3):
            to = lax.rem(y + d, NY)
            copies.append(
                pltpu.make_async_remote_copy(
                    src_ref=msg.at[to], dst_ref=mid.at[y], send_sem=near_send.at[k, d - 1], recv_sem=near_recv.at[k, d - 1],
                    device_id=(to * NW + w, q), device_id_type=MESH,
                )
            )
        return copies

    def across(src, dst, k):
        def step(d, carry):
            to = lax.rem(w + 1 + lax.rem(d + 7, NW - 1), NW)
            pltpu.make_async_remote_copy(
                src_ref=src(to), dst_ref=dst(w), send_sem=wide_send.at[k], recv_sem=wide_recv.at[k],
                device_id=(y * NW + to, q), device_id_type=MESH,
            ).start()
            return carry

        lax.fori_loop(0, NW - 1, step, 0)

    most = pl.ds(0, NW - 1)
    first_a = along_y(msg_a, mid_a, 0)
    for copy in first_a:
        copy.start()
    for copies in scatter:
        for copy in copies:
            copy.start()

    loads[15].wait()
    loads[16].wait()

    def cut(i, carry):
        here = pl.ds(pl.multiple_of(i * 128, 128), 128)
        there = pl.ds(pl.multiple_of(i * LAYERS, LAYERS), LAYERS)
        fields[0, there, :] = beside(species[0, :, here])
        for k in range(3):
            fields[k + 1, there, :] = beside(flow[k, :, here])
        return carry

    mid_a[y] = msg_a[y]
    for copy in first_a:
        copy.wait_recv()
    packed = pack_a.reshape(NW * NW, 128)
    for src in range(NY):
        for k in range(KINDS):
            packed[pl.ds(src * KINDS + k, NW, stride=NW), :] = mid_a[src, k]
    rows_a = pl.ds(0, NY * KINDS)
    across(lambda to: pack_a.at[to, rows_a], lambda me: recv_a.at[me, rows_a], 0)
    recv_a[w] = pack_a[w]
    addressed(
        [to_slot, high + 6.0, low + 7.0],
        [table[...], jnp.where(left, up0, up1), jnp.where(left, lo0, lo1)],
        msg_b.reshape(NB * ROWS, 128),
    )
    keep_b = pltpu.make_async_copy(msg_b.at[y], mid_b.at[y], local_sems.at[0])
    first_b = along_y(msg_b, mid_b, 1)
    keep_b.start()
    for copy in first_b:
        copy.start()

    lax.fori_loop(0, CUT, cut, 0, unroll=2)
    lax.fori_loop(CUT, LAYERS, cut, 0, unroll=2)

    keep_b.wait()
    for copy in first_b:
        copy.wait_recv()
    across(lambda to: mid_b.at[:, to], lambda me: parcels.at[:, me], 1)
    keep_b = pltpu.make_async_copy(mid_b.at[:, w], parcels.at[:, w], local_sems.at[1])
    keep_b.start()

    def gather_part(c):
        for copy in scatter[c]:
            copy.wait_recv()
        total = (z_part[q, :, part[c]] + z_got[0, :, part[c]]) + (z_got[1, :, part[c]] + z_got[2, :, part[c]])
        z_mine[:, part[c]] = total
        for copy in gather[c]:
            copy.start()
        z_sum[q, :, part[c]] = total

    pltpu.make_async_copy(recv_a.at[most, rows_a], recv_a.at[most, rows_a], wide_recv.at[0]).wait()
    got = recv_a.reshape(NW * NW, 128)
    own, own_z, own_edges = (
        jnp.concatenate([got[pl.ds(src * KINDS + k, NW, stride=NW), :] for src in range(NY)], axis=0) for k in range(KINDS)
    )
    forward[q, 0] = own
    forward[q, 1] = own_z
    onward = [sp_copy(forward.at[q], forward.at[q], 2 * CHUNKS, d) for d in (2, 1, 3)]
    for copy in onward:
        copy.start()
    gather_part(0)

    got_b = parcels.reshape(NB * ROWS, 128)
    own_cells = jnp.concatenate([own[:, 8 * r : 8 * r + 1] for r in range(CAP)], axis=0)
    speeds = list(lookups(own_cells, fields, (1, 2, 3)))

    @pl.when(q != 0)
    def _():
        for c in range(1, CHUNKS):
            gather_part(c)

    for copy in onward:
        copy.wait_recv()
    meta = jnp.concatenate([forward[k, 0] for k in range(NQ)], axis=0)
    shared = [
        pltpu.make_async_remote_copy(
            src_ref=fuel, dst_ref=fuel, send_sem=fuel_send.at[d - 1], recv_sem=fuel_recv, device_id=(b, d), device_id_type=MESH
        )
        for d in (2, 1, 3)
    ]

    @pl.when(q == 0)
    def _():
        lane = iota((NB * NQ, 128), 1)
        found = jnp.zeros((NB * NQ, 128), F32)
        cells = jnp.concatenate([meta[:, 8 * r : 8 * r + 1] for r in range(CAP)], axis=0)
        [value] = lookups(cells, fields, (0,))
        for r in range(CAP):
            found = jnp.where(lane == r, value[r * NB * NQ : (r + 1) * NB * NQ], found)
        fuel[...] = jnp.transpose(found)[:8]
        for copy in shared:
            copy.start()
        for c in range(1, CHUNKS):
            gather_part(c)

    meta_t = jnp.transpose(meta)
    cells = jnp.concatenate([meta_t[8 * r : 8 * r + 1, :] for r in range(CAP)], axis=1).astype(jnp.int32)
    row = ((cells & 4095) >> 7) * LAYERS + (cells >> 12)
    for m in range(4):
        hot[m * 256 : (m + 1) * 256, :] = ones(iota((256, NB * NQ * CAP), 0) + m * 256 == row)

    def fill_ghosts():
        keep_b.wait()
        pltpu.make_async_copy(parcels.at[:, most], parcels.at[:, most], wide_recv.at[1]).wait()
        low_sel = ones(iota((NB, NB), 1).astype(F32) == column(lp[...].astype(F32)))
        high_sel = ones(iota((NB, NB), 1).astype(F32) == column(hp[...].astype(F32)))
        z_tiles = (forward[0, 1] + forward[1, 1]) + (forward[2, 1] + forward[3, 1])
        below = pick_rows(low_sel, jnp.concatenate([got_b[pl.ds(6, NB, stride=ROWS), :], z_tiles], axis=1))
        above = pick_rows(
            high_sel, jnp.concatenate([got_b[pl.ds(7, NB, stride=ROWS), :], own_edges, z_tiles], axis=1)
        )
        tiles = jnp.concatenate([below[:, :128], above[:, :128], above[:, 128:256], jnp.where(left, below[:, 128:], above[:, 256:])], axis=0)
        spread_tiles = mm(beside(tiles), spread[...])
        mask = strip_mask()
        slots = ((0, 1), (3, 4), (6, 7), (2, 5))
        for g in range(4):
            for jt in range(8):
                strip = spread_tiles[g * 64 + jt * 8 : g * 64 + jt * 8 + 8]
                for side in range(2):
                    value = jnp.sum(jnp.where(mask, strip[:, side * 512 : (side + 1) * 512], 0.0), axis=0, keepdims=True)
                    ghosts[slots[g][side] : slots[g][side] + 1, jt * 512 : (jt + 1) * 512] = value

    fill_ghosts()

    @pl.when(q != 0)
    def _():
        shared[0].wait_recv()

    found_col = jnp.transpose(jnp.concatenate([fuel[...], jnp.zeros((120, NB * NQ), F32)], axis=0))
    fuel_col[...] = found_col
    lane = iota((NB * NQ, 128), 1)
    mass = []
    for r in range(CAP):
        k = 8 * r
        gone = meta[:, k + 1 : k + 2] * (meta[:, k + 2 : k + 3] - found_col[:, r : r + 1])
        at = meta[:, k : k + 1].astype(jnp.int32) & 127
        mass.append(beside(jnp.where(lane == at, gone, 0.0)))
    source[...] = folded(mm(hot[...], jnp.concatenate(mass, axis=0)), 128)

    own_fuel = fuel_col[pl.ds(pl.multiple_of(q * NB, NB), NB), :]
    lane = iota((NB, 128), 1)
    for r in range(CAP):
        k = 8 * r
        gone = own[:, k + 1 : k + 2] * (own[:, k + 2 : k + 3] - own_fuel[:, r : r + 1])
        drag = DRAG * own[:, k + 3 : k + 4]
        moved = jnp.where(lane == 0, -gone, 0.0)
        for c in range(3):
            moved = jnp.where(lane == 3 + c, drag * speeds[c][r * NB : (r + 1) * NB], moved)
        change[pl.ds(r, NB, stride=CAP), :] = moved

    @pl.when(q == 0)
    def _():
        for copy in shared:
            copy.wait_send()

    pltpu.make_async_copy(pack_a.at[most, rows_a], pack_a.at[most, rows_a], wide_send.at[0]).wait()
    pltpu.make_async_copy(mid_b.at[:, most], mid_b.at[:, most], wide_send.at[1]).wait()
    for copy in first_a + first_b:
        copy.wait_send()
    for copies in scatter:
        for copy in copies:
            copy.wait_send()
    for copy in onward:
        copy.wait_send()
    for copies in gather:
        for copy in copies:
            copy.wait()


def final_kernel(
    dif, species, flow, diffusion, inv_volume, z_sum, source, ghosts, parcels, change, new_species, arrived, out, landed, out_sems,
):
    q = lax.axis_index("sp")
    d = (dif[0], dif[1])
    lane = iota((NB, 128), 1)
    keep = jnp.where((lane >= 3) & (lane <= 5), 1.0 - DRAG, 1.0)
    for r in range(CAP):
        landed[pl.ds(r, NB, stride=CAP), :] = parcels[pl.ds(r, NB, stride=ROWS), :] * keep + change[pl.ds(r, NB, stride=CAP), :]

    writes = [pltpu.make_async_copy(landed, arrived, out_sems.at[0])]
    writes[0].start()

    lane = iota((LAYERS, 128), 1)
    layer = iota((LAYERS, 128), 0)
    fuel = jnp.where(q == 0, 1.0, 0.0)
    right_half = lane >= 64
    inside = (lane & 63) != 0

    def strip(n, carry):
        i = LAYERS - 1 - n
        here = pl.ds(pl.multiple_of(i * 128, 128), 128)
        back = pl.ds(pl.multiple_of(jnp.maximum(i - 1, 0) * 128, 128), 128)
        beyond_wall = (i > 0) | right_half

        def below_of(x, ghost):
            return jnp.where(layer == 0, ghost, pltpu.roll(x, 1, 0))

        def before_of(x, previous):
            return pltpu.roll(jnp.where(right_half, previous, x), 64, 1)

        z = z_sum[:, here]
        g0, g1, g2 = diffusion[0, :, here], diffusion[1, :, here], diffusion[2, :, here]
        gt = ghosts[7:8, here]
        h0 = 0.5 * (flow[0, :, here] + g0 * (z - below_of(z, ghosts[2:3, here])))
        ht = 0.5 * (ghosts[6:7, here] + gt * (ghosts[5:6, here] - z[LAYERS - 1 :]))
        h1 = 0.5 * (flow[1, :, here] + g1 * (z - before_of(z, z_sum[:, back])))
        h2 = 0.5 * (flow[2, :, here] + g2 * (z - pltpu.roll(z, 1, 1)))
        h1, g1 = jnp.where(beyond_wall, h1, 0.0), jnp.where(beyond_wall, g1, 0.0)
        h2, g2 = jnp.where(inside, h2, 0.0), jnp.where(inside, g2, 0.0)
        half_inv = STEP * inv_volume[:, here]
        src = source[pl.ds(pl.multiple_of(i * LAYERS, LAYERS), LAYERS), :]
        onward = []
        for s in range(2):
            y = species[s, :, here]
            top = ghosts[3 + s : 4 + s, here]
            last = y[LAYERS - 1 :]
            y0 = below_of(y, ghosts[s : s + 1, here])
            y1 = before_of(y, species[s, :, back])
            y2 = pltpu.roll(y, 1, 1)
            f0 = h0 * (y + y0) - (g0 * d[s]) * (y - y0)
            ft = ht * (top + last) - (gt * d[s]) * (top - last)
            f1 = h1 * (y + y1) - (g1 * d[s]) * (y - y1)
            f2 = h2 * (y + y2) - (g2 * d[s]) * (y - y2)
            u0 = jnp.where(layer == LAYERS - 1, ft, pltpu.roll(f0, LAYERS - 1, 0))
            u1 = pltpu.roll(jnp.where(right_half, f1, carry[s]), 64, 1)
            u2 = pltpu.roll(f2, 127, 1)
            divergence = (u0 - f0) + ((u1 - f1) + (u2 - f2))
            delta = fuel if s == 0 else 0.0
            out[s, :, here] = y + half_inv * (src * (delta - y) - divergence)
            onward.append(f1)
        return tuple(onward)

    carry = (jnp.zeros((LAYERS, 128), F32),) * 2
    bounds = (0, 8, 16, 24, 28, 32)
    for g in range(5):
        carry = lax.fori_loop(bounds[g], bounds[g + 1], strip, carry, unroll=4)
        done = pl.ds((LAYERS - bounds[g + 1]) * 128, (bounds[g + 1] - bounds[g]) * 128)
        writes.append(pltpu.make_async_copy(out.at[:, :, done], new_species.at[:, :, done], out_sems.at[g + 1]))
        writes[-1].start()
    for write in writes:
        write.wait()


def spec(space=pltpu.VMEM):
    return pl.BlockSpec(memory_space=space)


HBM = pl.BlockSpec(memory_space=pltpu.HBM)


def params(**kw):
    return pltpu.CompilerParams(vmem_limit_bytes=VMEM_LIMIT, **kw)


def shape(*dims):
    return jax.ShapeDtypeStruct(dims, F32)


def body(
    species, interface_normal_flow, face_diffusion, inv_volume, diffusivity, low_partner, high_partner,
    low_orient, high_orient, droplet_table, parcel_block, parcel_cell, parcel_live,
):
    pick, oriented, unoriented, spread = constants()
    dma = pltpu.SemaphoreType.DMA
    vm = lambda *dims: pltpu.VMEM(dims, F32)
    iv = lambda *dims: pltpu.VMEM(dims, jnp.int32)
    bv = lambda *dims: pltpu.VMEM(dims, BF16)
    z_sum, source, ghosts, parcels, change = pl.pallas_call(
        exchange_kernel,
        out_shape=(shape(NQ, 8, JK), shape(1024, 128), shape(8, JK), shape(NY, NW, ROWS, 128), shape(NB * CAP, 128)),
        in_specs=[HBM] * 16,
        out_specs=(spec(),) * 5,
        scratch_shapes=[
            pltpu.SMEM((2,), F32), vm(2, LAYERS, JK), vm(3, LAYERS, JK), vm(2, 8, JK), *[iv(1, 64)] * 4, vm(256, 128), *[iv(1, 256)] * 3,
            bv(1536, 192), bv(192, 1024), bv(192, 1024), bv(384, 1024),
            vm(NY, KINDS, NW, 128), vm(NY, NW, ROWS, 128), vm(NY, KINDS, NW, 128), vm(NY, NW, ROWS, 128), *[vm(NW, NW, 128)] * 2,
            vm(NQ, 2, NB, 128),
            vm(NQ, 8, JK), vm(3, 8, JK), vm(8, JK), vm(8, 256), vm(256, 128), bv(4, 1024, 384), bv(1024, 1536),
            dma((17,)), dma((2 * CHUNKS + 1, 3)), dma((2 * CHUNKS + 1, 3)), dma((2, 3)), dma((2, 3)), dma((2,)), dma((2,)), dma((2,)), dma((3,)), dma,
        ],
        compiler_params=params(collective_id=0, has_side_effects=True),
        name="exchange",
    )(*(pltpu.with_memory_space_constraint(x, pltpu.HBM) for x in (
        diffusivity, species, interface_normal_flow, face_diffusion, low_partner, high_partner, low_orient, high_orient,
        droplet_table, parcel_block.reshape(1, -1), parcel_cell.reshape(1, -1), parcel_live.reshape(1, -1),
        pick, oriented, unoriented, spread,
    )))
    new_species, arrived = pl.pallas_call(
        final_kernel,
        out_shape=(shape(2, LAYERS, JK), shape(384, 128)),
        in_specs=[pl.BlockSpec(memory_space=pltpu.SMEM)] + [spec()] * 9,
        out_specs=(HBM, HBM),
        scratch_shapes=[vm(2, LAYERS, JK), vm(NB * CAP, 128), dma((6,))],
        compiler_params=params(),
        name="final",
    )(
        diffusivity, species, interface_normal_flow, face_diffusion, inv_volume, z_sum.reshape(LAYERS, JK), source, ghosts,
        parcels.reshape(NB * ROWS, 128), change,
    )
    return new_species, arrived


def solution(mesh):
    placed = (
        P("sp", "blk", None), P(None, "blk", None), P(None, "blk", None), P("blk", None), P("sp"),
        P("blk", None), P("blk", None), P("blk", None), P("blk", None),
        P(("blk", "sp"), None), P(("blk", "sp"), None), P(("blk", "sp")), P(("blk", "sp")),
    )
    return jax.shard_map(
        body, mesh=mesh, in_specs=placed, out_specs=(P("sp", "blk", None), P(("blk", "sp"), None)), check_vma=False,
    )
```

```python
import functools
import jax
import jax.numpy as jnp
import numpy as np
from jax import lax
from jax.experimental import pallas as pl
from jax.experimental.pallas import tpu as pltpu
from jax.sharding import PartitionSpec as P

NB = 64
NQ = 4
CAP = 6
ROWS = 8
CHUNKS = 2
NY = 4
NW = 16
CUT = 16
KINDS = 3
LAYERS = 32
JK = 4096
MESH = pl.DeviceIdType.MESH
F32 = jnp.float32
BF16 = jnp.bfloat16
STEP = 0.5
DRAG = 0.3
VMEM_LIMIT = 36 * 1024 * 1024


def constants():
    lane = np.arange(512)
    cell = np.arange(64)
    pick = (lane[:, None] // 64 == cell[None, :] // 8) & (lane[:, None] % 8 == cell[None, :] % 8)
    r, c = cell // 8, cell % 8
    oriented, unoriented = [], []
    for code in range(8):
        f_row = (lambda v: 7 - v) if code & 1 else (lambda v: v)
        f_col = (lambda v: 7 - v) if code & 2 else (lambda v: v)
        r2, c2 = f_row(r), f_col(c)
        source = c2 * 8 + r2 if code & 4 else r2 * 8 + c2
        oriented += [cell[:, None] == source[None, :]] * 2
        source = f_row(c) * 8 + f_col(r) if code & 4 else f_row(r) * 8 + f_col(c)
        unoriented += [cell[:, None] == source[None, :]] * 2
    spread = np.zeros((128, 1024), bool)
    spread[:64, :512] = pick.T
    spread[64:, 512:] = pick.T
    pick3 = np.zeros((1536, 192), bool)
    for k in range(3):
        pick3[k * 512 : (k + 1) * 512, k * 64 : (k + 1) * 64] = pick
    thrice = lambda m: np.concatenate([m] * 3, 0)
    asb = lambda m: jnp.asarray(m.astype(np.float32), BF16)
    return asb(pick3), asb(thrice(np.concatenate(oriented, 1))), asb(thrice(np.concatenate(unoriented, 1))), asb(thrice(spread))


def pieces(x):
    hi = x.astype(BF16)
    rest = x - hi.astype(F32)
    mid = rest.astype(BF16)
    low = (rest - mid.astype(F32)).astype(BF16)
    return hi, mid, low


def mm(a, b):
    return lax.dot_general(a, b, (((1,), (0,)), ((), ())), preferred_element_type=F32)


def beside(x):
    return jnp.concatenate(pieces(x), axis=1)


def folded(x, n):
    return (x[:, :n] + x[:, n : 2 * n]) + x[:, 2 * n :]


def pick_rows(onehot, x):
    return folded(mm(onehot, beside(x)), x.shape[1])


def iota(shape, axis):
    return lax.broadcasted_iota(jnp.int32, shape, axis)


def ones(mask):
    return jnp.where(mask, 1.0, 0.0).astype(BF16)


def column(row):
    n = row.shape[1]
    return jnp.sum(jnp.where(iota((n, n), 0) == iota((n, n), 1), row, 0.0), axis=1, keepdims=True)


def strip_mask():
    lane = iota((8, 512), 1)
    return (lane % 64) // 8 == iota((8, 512), 0)


def stack_field(ref_slice):
    return jnp.concatenate([ref_slice[:, i * 128 : (i + 1) * 128] for i in range(LAYERS)], axis=0)


def lookups(cells, fields, ks):
    n = cells.shape[0]
    whole = cells.astype(jnp.int32)
    row = ((whole & 4095) >> 7) * LAYERS + (whole >> 12)
    hot = ones(iota((n, 1024), 1) == row)
    here = iota((n, 128), 1) == (whole & 127)
    for k in ks:
        yield jnp.sum(jnp.where(here, folded(mm(hot, fields[k]), 128), 0.0), axis=1, keepdims=True)


def ranks(block, live):
    n = block.shape[1]
    alive = live[...] == 1
    target = block[...].astype(F32)
    key = jnp.where(alive, target, -1.0)
    key_col = column(key)
    same = key_col == key
    first, second = iota((n, n), 0), iota((n, n), 1)
    rank = jnp.sum(jnp.where(same & (first < second), 1.0, 0.0), axis=0, keepdims=True)
    rank_col = jnp.sum(jnp.where(same & (second < first), 1.0, 0.0), axis=1, keepdims=True)
    return jnp.where(alive, target * ROWS, -1.0), jnp.where(alive, target * ROWS + rank, -1.0), rank_col


def meta_rows(table, cell, rank_col):
    rows = table[...]
    lane = iota(rows.shape, 1)
    cell_col = column(cell[...].astype(F32))
    boil = jnp.maximum(rows, 0.0) + jnp.log1p(jnp.exp(-jnp.abs(rows)))
    sig = 1.0 / (1.0 + jnp.exp(-rows))
    kind = lane & 7
    meta = jnp.where(kind == 0, cell_col, jnp.where(kind == 1, boil[:, 1:2], jnp.where(kind == 2, sig[:, 2:3], jnp.where(kind == 3, 1.0, 0.0))))
    return jnp.where((lane >> 3).astype(F32) == rank_col, meta, 0.0)


def turned_tiles(faces, pick, oriented, unoriented, high_code, low_code):
    mask = strip_mask()
    strips = []
    for face in faces:
        for jt in range(8):
            strips.append(jnp.where(mask, face[:, jt * 512 : (jt + 1) * 512], 0.0))
    tiles = mm(beside(jnp.concatenate(strips, axis=0)), pick[...]).astype(BF16)
    turned = mm(tiles[:128], oriented[...])
    unturned = mm(tiles[128:], unoriented[...])

    def choose(x, code):
        out = x[:, :128]
        for o in range(1, 8):
            out = jnp.where(code == o, x[:, o * 128 : (o + 1) * 128], out)
        return out

    return [choose(turned[k * 64 : (k + 1) * 64], high_code) for k in range(2)] + [
        choose(unturned[k * 64 : (k + 1) * 64], low_code) for k in range(4)
    ]


def addressed(keys, values, out):
    keys, values = jnp.concatenate(keys, axis=1), jnp.concatenate(values, axis=0)
    out[...] = pick_rows(ones(iota((NB * ROWS, keys.shape[1]), 0).astype(F32) == keys), values)


def exchange_kernel(
    dif_in, species_in, flow_in, diffusion_in, lp_in, hp_in, lo_in, ho_in, table_in, block_in, cell_in, live_in,
    pick_in, oriented_in, unoriented_in, spread_in,
    z_sum, source, ghosts, parcels, change,
    dif, species, flow, edge, lp, hp, lo, ho, table, block, cell, live, pick, oriented, unoriented, spread,
    msg_a, msg_b, mid_a, mid_b, pack_a, recv_a, lists, forward, z_part, z_got, z_mine, fuel, fuel_col, fields, hot,
    load_sems, sems, recv_sems, near_send, near_recv, wide_send, wide_recv, local_sems, fuel_send, fuel_recv,
):
    b, q = lax.axis_index("blk"), lax.axis_index("sp")
    y, w = lax.div(b, NW), lax.rem(b, NW)
    pairs = (
        (species_in, species), (dif_in, dif), (flow_in.at[0, pl.ds(0, 8)], edge.at[0]), (diffusion_in.at[0, pl.ds(0, 8)], edge.at[1]),
        (table_in, table), (block_in, block), (live_in, live), (cell_in, cell), (lp_in, lp), (hp_in, hp), (lo_in, lo), (ho_in, ho),
        (pick_in, pick), (oriented_in, oriented), (unoriented_in, unoriented), (flow_in, flow), (spread_in, spread),
    )
    loads = [pltpu.make_async_copy(src, dst, load_sems.at[k]) for k, (src, dst) in enumerate(pairs)]
    for load in loads:
        load.start()
    barrier = pltpu.get_barrier_semaphore()

    for d in range(1, NQ):
        pl.semaphore_signal(barrier, inc=1, device_id=(b, lax.rem(q + d, NQ)), device_id_type=MESH)
    for d in range(1, NY):
        pl.semaphore_signal(barrier, inc=1, device_id=(lax.rem(y + d, NY) * NW + w, q), device_id_type=MESH)
    for d in range(1, NW):
        pl.semaphore_signal(barrier, inc=1, device_id=(y * NW + lax.rem(w + d, NW), q), device_id_type=MESH)
    loads[0].wait()
    loads[1].wait()

    d0, d1 = dif[0], dif[1]
    for k in range(NQ):
        z_part[k] = d0 * species[0, k * 8 : (k + 1) * 8] + d1 * species[1, k * 8 : (k + 1) * 8]
    for load in loads[2:15]:
        load.wait()
    to_block, to_slot, rank_col = ranks(block, live)
    up0, up1, lo0, lo1, fl, df = turned_tiles(
        [
            species[0, LAYERS - 1 : LAYERS, :], species[1, LAYERS - 1 : LAYERS, :], species[0, 0:1, :], species[1, 0:1, :],
            edge[0, 0:1, :], edge[1, 0:1, :],
        ],
        pick, oriented, unoriented, column(ho[...].astype(F32)), column(lo[...].astype(F32)),
    )
    left = iota((NB, 128), 1) < 64
    high, low = hp[...].astype(F32) * ROWS, lp[...].astype(F32) * ROWS
    by_block = iota((NB, 256), 0).astype(F32) * ROWS == to_block
    tile_keys = jnp.concatenate([high, low], axis=1)
    by_tile = ones(iota((NB, 2 * NB), 0).astype(F32) * ROWS == tile_keys)
    z_tiles = jnp.concatenate([jnp.where(left, d0 * up0 + d1 * up1, 0.0), jnp.where(left, 0.0, d0 * lo0 + d1 * lo1)], axis=0)
    edges = jnp.concatenate([jnp.zeros((NB, 128), F32), jnp.where(left, fl, df)], axis=0)
    picked = pick_rows(by_tile, jnp.concatenate([z_tiles, edges], axis=1))
    kinds = (pick_rows(ones(by_block), meta_rows(table, cell, rank_col)), picked[:, :128], picked[:, 128:])
    for k in range(KINDS):
        for to in range(NY):
            msg_a[to, k] = kinds[k][to * NW : (to + 1) * NW]
    pl.semaphore_wait(barrier, NQ + NY + NW - 3)

    def sp_copy(src, dst, k, d):
        return pltpu.make_async_remote_copy(
            src_ref=src, dst_ref=dst, send_sem=sems.at[k, d - 1], recv_sem=recv_sems.at[k, d - 1],
            device_id=(b, lax.rem(q + d, NQ)), device_id_type=MESH,
        )

    wide = JK // CHUNKS
    part = [pl.ds(c * wide, wide) for c in range(CHUNKS)]
    scatter = [
        [sp_copy(z_part.at[lax.rem(q + d, NQ), :, part[c]], z_got.at[d - 1, :, part[c]], c, d) for d in (2, 1, 3)]
        for c in range(CHUNKS)
    ]
    gather = [
        [sp_copy(z_mine.at[:, part[c]], z_sum.at[q, :, part[c]], CHUNKS + c, d) for d in (2, 1, 3)] for c in range(CHUNKS)
    ]

    def along_y(msg, mid, k):
        copies = []
        for d in (2, 1, 3):
            to = lax.rem(y + d, NY)
            copies.append(
                pltpu.make_async_remote_copy(
                    src_ref=msg.at[to], dst_ref=mid.at[y], send_sem=near_send.at[k, d - 1], recv_sem=near_recv.at[k, d - 1],
                    device_id=(to * NW + w, q), device_id_type=MESH,
                )
            )
        return copies

    def across(src, dst, k):
        def step(d, carry):
            to = lax.rem(w + 1 + lax.rem(d + 7, NW - 1), NW)
            pltpu.make_async_remote_copy(
                src_ref=src(to), dst_ref=dst(w), send_sem=wide_send.at[k], recv_sem=wide_recv.at[k],
                device_id=(y * NW + to, q), device_id_type=MESH,
            ).start()
            return carry

        lax.fori_loop(0, NW - 1, step, 0)

    most = pl.ds(0, NW - 1)
    first_a = along_y(msg_a, mid_a, 0)
    for copy in first_a:
        copy.start()
    for copies in scatter:
        for copy in copies:
            copy.start()

    loads[15].wait()
    loads[16].wait()

    def cut(i, carry):
        here = pl.ds(pl.multiple_of(i * 128, 128), 128)
        there = pl.ds(pl.multiple_of(i * LAYERS, LAYERS), LAYERS)
        fields[0, there, :] = beside(species[0, :, here])
        for k in range(3):
            fields[k + 1, there, :] = beside(flow[k, :, here])
        return carry

    mid_a[y] = msg_a[y]
    for copy in first_a:
        copy.wait_recv()
    packed = pack_a.reshape(NW * NW, 128)
    for src in range(NY):
        for k in range(KINDS):
            packed[pl.ds(src * KINDS + k, NW, stride=NW), :] = mid_a[src, k]
    rows_a = pl.ds(0, NY * KINDS)
    across(lambda to: pack_a.at[to, rows_a], lambda me: recv_a.at[me, rows_a], 0)
    recv_a[w] = pack_a[w]
    addressed(
        [to_slot, high + 6.0, low + 7.0],
        [table[...], jnp.where(left, up0, up1), jnp.where(left, lo0, lo1)],
        msg_b.reshape(NB * ROWS, 128),
    )
    keep_b = pltpu.make_async_copy(msg_b.at[y], mid_b.at[y], local_sems.at[0])
    first_b = along_y(msg_b, mid_b, 1)
    keep_b.start()
    for copy in first_b:
        copy.start()

    lax.fori_loop(0, CUT, cut, 0, unroll=2)
    lax.fori_loop(CUT, LAYERS, cut, 0, unroll=2)

    keep_b.wait()
    for copy in first_b:
        copy.wait_recv()
    across(lambda to: mid_b.at[:, to], lambda me: parcels.at[:, me], 1)
    keep_b = pltpu.make_async_copy(mid_b.at[:, w], parcels.at[:, w], local_sems.at[1])
    keep_b.start()

    def gather_part(c):
        for copy in scatter[c]:
            copy.wait_recv()
        total = (z_part[q, :, part[c]] + z_got[0, :, part[c]]) + (z_got[1, :, part[c]] + z_got[2, :, part[c]])
        z_mine[:, part[c]] = total
        for copy in gather[c]:
            copy.start()
        z_sum[q, :, part[c]] = total

    pltpu.make_async_copy(recv_a.at[most, rows_a], recv_a.at[most, rows_a], wide_recv.at[0]).wait()
    got = recv_a.reshape(NW * NW, 128)
    own, own_z, own_edges = (
        jnp.concatenate([got[pl.ds(src * KINDS + k, NW, stride=NW), :] for src in range(NY)], axis=0) for k in range(KINDS)
    )
    lists[q] = jnp.where(iota((NB // 2, 128), 1) < 64, own[: NB // 2], pltpu.roll(own[NB // 2 :], 64, 1))
    forward[q] = own_z
    onward = [sp_copy(lists.at[q], lists.at[q], 2 * CHUNKS, d) for d in (2, 1, 3)]
    onward_z = [sp_copy(forward.at[q], forward.at[q], 2 * CHUNKS + 1, d) for d in (2, 1, 3)]
    for copy in onward + onward_z:
        copy.start()
    gather_part(0)

    got_b = parcels.reshape(NB * ROWS, 128)
    own_cells = jnp.concatenate([own[:, 8 * r : 8 * r + 1] for r in range(CAP)], axis=0)
    speeds = list(lookups(own_cells, fields, (1, 2, 3)))

    @pl.when(q != 0)
    def _():
        for c in range(1, CHUNKS):
            gather_part(c)

    for copy in onward:
        copy.wait_recv()
    meta = []
    for k in range(NQ):
        both = lists[k]
        meta += [both, pltpu.roll(both, 64, 1)]
    meta = jnp.concatenate(meta, axis=0)
    shared = [
        pltpu.make_async_remote_copy(
            src_ref=fuel, dst_ref=fuel, send_sem=fuel_send.at[d - 1], recv_sem=fuel_recv, device_id=(b, d), device_id_type=MESH
        )
        for d in (2, 1, 3)
    ]

    @pl.when(q == 0)
    def _():
        lane = iota((NB * NQ, 128), 1)
        found = jnp.zeros((NB * NQ, 128), F32)
        cells = jnp.concatenate([meta[:, 8 * r : 8 * r + 1] for r in range(CAP)], axis=0)
        [value] = lookups(cells, fields, (0,))
        for r in range(CAP):
            found = jnp.where(lane == r, value[r * NB * NQ : (r + 1) * NB * NQ], found)
        fuel[...] = jnp.transpose(found)[:8]
        for copy in shared:
            copy.start()
        for c in range(1, CHUNKS):
            gather_part(c)

    meta_t = jnp.transpose(meta)
    cells = jnp.concatenate([meta_t[8 * r : 8 * r + 1, :] for r in range(CAP)], axis=1).astype(jnp.int32)
    row = ((cells & 4095) >> 7) * LAYERS + (cells >> 12)
    for m in range(4):
        hot[m * 256 : (m + 1) * 256, :] = ones(iota((256, NB * NQ * CAP), 0) + m * 256 == row)

    def fill_ghosts():
        keep_b.wait()
        pltpu.make_async_copy(parcels.at[:, most], parcels.at[:, most], wide_recv.at[1]).wait()
        low_sel = ones(iota((NB, NB), 1).astype(F32) == column(lp[...].astype(F32)))
        high_sel = ones(iota((NB, NB), 1).astype(F32) == column(hp[...].astype(F32)))
        for copy in onward_z:
            copy.wait_recv()
        z_tiles = (forward[0] + forward[1]) + (forward[2] + forward[3])
        below = pick_rows(low_sel, jnp.concatenate([got_b[pl.ds(6, NB, stride=ROWS), :], z_tiles], axis=1))
        above = pick_rows(
            high_sel, jnp.concatenate([got_b[pl.ds(7, NB, stride=ROWS), :], own_edges, z_tiles], axis=1)
        )
        tiles = jnp.concatenate([below[:, :128], above[:, :128], above[:, 128:256], jnp.where(left, below[:, 128:], above[:, 256:])], axis=0)
        spread_tiles = mm(beside(tiles), spread[...])
        mask = strip_mask()
        slots = ((0, 1), (3, 4), (6, 7), (2, 5))
        for g in range(4):
            for jt in range(8):
                strip = spread_tiles[g * 64 + jt * 8 : g * 64 + jt * 8 + 8]
                for side in range(2):
                    value = jnp.sum(jnp.where(mask, strip[:, side * 512 : (side + 1) * 512], 0.0), axis=0, keepdims=True)
                    ghosts[slots[g][side] : slots[g][side] + 1, jt * 512 : (jt + 1) * 512] = value

    fill_ghosts()

    @pl.when(q != 0)
    def _():
        shared[0].wait_recv()

    found_col = jnp.transpose(jnp.concatenate([fuel[...], jnp.zeros((120, NB * NQ), F32)], axis=0))
    fuel_col[...] = found_col
    lane = iota((NB * NQ, 128), 1)
    mass = []
    for r in range(CAP):
        k = 8 * r
        gone = meta[:, k + 1 : k + 2] * (meta[:, k + 2 : k + 3] - found_col[:, r : r + 1])
        at = meta[:, k : k + 1].astype(jnp.int32) & 127
        mass.append(beside(jnp.where(lane == at, gone, 0.0)))
    source[...] = folded(mm(hot[...], jnp.concatenate(mass, axis=0)), 128)

    own_fuel = fuel_col[pl.ds(pl.multiple_of(q * NB, NB), NB), :]
    lane = iota((NB, 128), 1)
    for r in range(CAP):
        k = 8 * r
        gone = own[:, k + 1 : k + 2] * (own[:, k + 2 : k + 3] - own_fuel[:, r : r + 1])
        drag = DRAG * own[:, k + 3 : k + 4]
        moved = jnp.where(lane == 0, -gone, 0.0)
        for c in range(3):
            moved = jnp.where(lane == 3 + c, drag * speeds[c][r * NB : (r + 1) * NB], moved)
        change[pl.ds(r, NB, stride=CAP), :] = moved

    @pl.when(q == 0)
    def _():
        for copy in shared:
            copy.wait_send()

    pltpu.make_async_copy(pack_a.at[most, rows_a], pack_a.at[most, rows_a], wide_send.at[0]).wait()
    pltpu.make_async_copy(mid_b.at[:, most], mid_b.at[:, most], wide_send.at[1]).wait()
    for copy in first_a + first_b:
        copy.wait_send()
    for copies in scatter:
        for copy in copies:
            copy.wait_send()
    for copy in onward + onward_z:
        copy.wait_send()
    for copies in gather:
        for copy in copies:
            copy.wait()


def final_kernel(
    dif, species, flow, diffusion, inv_volume, z_sum, source, ghosts, parcels, change, new_species, arrived, out, landed, out_sems,
):
    q = lax.axis_index("sp")
    d = (dif[0], dif[1])
    lane = iota((NB, 128), 1)
    keep = jnp.where((lane >= 3) & (lane <= 5), 1.0 - DRAG, 1.0)
    for r in range(CAP):
        landed[pl.ds(r, NB, stride=CAP), :] = parcels[pl.ds(r, NB, stride=ROWS), :] * keep + change[pl.ds(r, NB, stride=CAP), :]

    writes = [pltpu.make_async_copy(landed, arrived, out_sems.at[0])]
    writes[0].start()

    lane = iota((LAYERS, 128), 1)
    layer = iota((LAYERS, 128), 0)
    fuel = jnp.where(q == 0, 1.0, 0.0)
    right_half = lane >= 64
    inside = (lane & 63) != 0

    def strip(n, carry):
        i = LAYERS - 1 - n
        here = pl.ds(pl.multiple_of(i * 128, 128), 128)
        back = pl.ds(pl.multiple_of(jnp.maximum(i - 1, 0) * 128, 128), 128)
        beyond_wall = (i > 0) | right_half

        def below_of(x, ghost):
            return jnp.where(layer == 0, ghost, pltpu.roll(x, 1, 0))

        def before_of(x, previous):
            return pltpu.roll(jnp.where(right_half, previous, x), 64, 1)

        z = z_sum[:, here]
        g0, g1, g2 = diffusion[0, :, here], diffusion[1, :, here], diffusion[2, :, here]
        gt = ghosts[7:8, here]
        h0 = 0.5 * (flow[0, :, here] + g0 * (z - below_of(z, ghosts[2:3, here])))
        ht = 0.5 * (ghosts[6:7, here] + gt * (ghosts[5:6, here] - z[LAYERS - 1 :]))
        h1 = 0.5 * (flow[1, :, here] + g1 * (z - before_of(z, z_sum[:, back])))
        h2 = 0.5 * (flow[2, :, here] + g2 * (z - pltpu.roll(z, 1, 1)))
        h1, g1 = jnp.where(beyond_wall, h1, 0.0), jnp.where(beyond_wall, g1, 0.0)
        h2, g2 = jnp.where(inside, h2, 0.0), jnp.where(inside, g2, 0.0)
        half_inv = STEP * inv_volume[:, here]
        src = source[pl.ds(pl.multiple_of(i * LAYERS, LAYERS), LAYERS), :]
        onward = []
        for s in range(2):
            y = species[s, :, here]
            top = ghosts[3 + s : 4 + s, here]
            last = y[LAYERS - 1 :]
            y0 = below_of(y, ghosts[s : s + 1, here])
            y1 = before_of(y, species[s, :, back])
            y2 = pltpu.roll(y, 1, 1)
            f0 = h0 * (y + y0) - (g0 * d[s]) * (y - y0)
            ft = ht * (top + last) - (gt * d[s]) * (top - last)
            f1 = h1 * (y + y1) - (g1 * d[s]) * (y - y1)
            f2 = h2 * (y + y2) - (g2 * d[s]) * (y - y2)
            u0 = jnp.where(layer == LAYERS - 1, ft, pltpu.roll(f0, LAYERS - 1, 0))
            u1 = pltpu.roll(jnp.where(right_half, f1, carry[s]), 64, 1)
            u2 = pltpu.roll(f2, 127, 1)
            divergence = (u0 - f0) + ((u1 - f1) + (u2 - f2))
            delta = fuel if s == 0 else 0.0
            out[s, :, here] = y + half_inv * (src * (delta - y) - divergence)
            onward.append(f1)
        return tuple(onward)

    carry = (jnp.zeros((LAYERS, 128), F32),) * 2
    bounds = (0, 8, 16, 24, 28, 32)
    for g in range(5):
        carry = lax.fori_loop(bounds[g], bounds[g + 1], strip, carry, unroll=4)
        done = pl.ds((LAYERS - bounds[g + 1]) * 128, (bounds[g + 1] - bounds[g]) * 128)
        writes.append(pltpu.make_async_copy(out.at[:, :, done], new_species.at[:, :, done], out_sems.at[g + 1]))
        writes[-1].start()
    for write in writes:
        write.wait()


def spec(space=pltpu.VMEM):
    return pl.BlockSpec(memory_space=space)


HBM = pl.BlockSpec(memory_space=pltpu.HBM)


def params(**kw):
    return pltpu.CompilerParams(vmem_limit_bytes=VMEM_LIMIT, **kw)


def shape(*dims):
    return jax.ShapeDtypeStruct(dims, F32)


def body(
    species, interface_normal_flow, face_diffusion, inv_volume, diffusivity, low_partner, high_partner,
    low_orient, high_orient, droplet_table, parcel_block, parcel_cell, parcel_live,
):
    pick, oriented, unoriented, spread = constants()
    dma = pltpu.SemaphoreType.DMA
    vm = lambda *dims: pltpu.VMEM(dims, F32)
    iv = lambda *dims: pltpu.VMEM(dims, jnp.int32)
    bv = lambda *dims: pltpu.VMEM(dims, BF16)
    z_sum, source, ghosts, parcels, change = pl.pallas_call(
        exchange_kernel,
        out_shape=(shape(NQ, 8, JK), shape(1024, 128), shape(8, JK), shape(NY, NW, ROWS, 128), shape(NB * CAP, 128)),
        in_specs=[HBM] * 16,
        out_specs=(spec(),) * 5,
        scratch_shapes=[
            pltpu.SMEM((2,), F32), vm(2, LAYERS, JK), vm(3, LAYERS, JK), vm(2, 8, JK), *[iv(1, 64)] * 4, vm(256, 128), *[iv(1, 256)] * 3,
            bv(1536, 192), bv(192, 1024), bv(192, 1024), bv(384, 1024),
            vm(NY, KINDS, NW, 128), vm(NY, NW, ROWS, 128), vm(NY, KINDS, NW, 128), vm(NY, NW, ROWS, 128), *[vm(NW, NW, 128)] * 2,
            vm(NQ, NB // 2, 128), vm(NQ, NB, 128),
            vm(NQ, 8, JK), vm(3, 8, JK), vm(8, JK), vm(8, 256), vm(256, 128), bv(4, 1024, 384), bv(1024, 1536),
            dma((17,)), dma((2 * CHUNKS + 2, 3)), dma((2 * CHUNKS + 2, 3)), dma((2, 3)), dma((2, 3)), dma((2,)), dma((2,)), dma((2,)), dma((3,)), dma,
        ],
        compiler_params=params(collective_id=0, has_side_effects=True),
        name="exchange",
    )(*(pltpu.with_memory_space_constraint(x, pltpu.HBM) for x in (
        diffusivity, species, interface_normal_flow, face_diffusion, low_partner, high_partner, low_orient, high_orient,
        droplet_table, parcel_block.reshape(1, -1), parcel_cell.reshape(1, -1), parcel_live.reshape(1, -1),
        pick, oriented, unoriented, spread,
    )))
    new_species, arrived = pl.pallas_call(
        final_kernel,
        out_shape=(shape(2, LAYERS, JK), shape(384, 128)),
        in_specs=[pl.BlockSpec(memory_space=pltpu.SMEM)] + [spec()] * 9,
        out_specs=(HBM, HBM),
        scratch_shapes=[vm(2, LAYERS, JK), vm(NB * CAP, 128), dma((6,))],
        compiler_params=params(),
        name="final",
    )(
        diffusivity, species, interface_normal_flow, face_diffusion, inv_volume, z_sum.reshape(LAYERS, JK), source, ghosts,
        parcels.reshape(NB * ROWS, 128), change,
    )
    return new_species, arrived


def solution(mesh):
    placed = (
        P("sp", "blk", None), P(None, "blk", None), P(None, "blk", None), P("blk", None), P("sp"),
        P("blk", None), P("blk", None), P("blk", None), P("blk", None),
        P(("blk", "sp"), None), P(("blk", "sp"), None), P(("blk", "sp")), P(("blk", "sp")),
    )
    return jax.shard_map(
        body, mesh=mesh, in_specs=placed, out_specs=(P("sp", "blk", None), P(("blk", "sp"), None)), check_vma=False,
    )
```

```python
import functools
import jax
import jax.numpy as jnp
import numpy as np
from jax import lax
from jax.experimental import pallas as pl
from jax.experimental.pallas import tpu as pltpu
from jax.sharding import PartitionSpec as P

NB = 64
NQ = 4
CAP = 6
ROWS = 8
CHUNKS = 2
NY = 4
NW = 16
CUT = 16
KINDS = 3
LAYERS = 32
JK = 4096
MESH = pl.DeviceIdType.MESH
F32 = jnp.float32
BF16 = jnp.bfloat16
STEP = 0.5
DRAG = 0.3
VMEM_LIMIT = 36 * 1024 * 1024


def constants():
    lane = np.arange(512)
    cell = np.arange(64)
    pick = (lane[:, None] // 64 == cell[None, :] // 8) & (lane[:, None] % 8 == cell[None, :] % 8)
    r, c = cell // 8, cell % 8
    oriented, unoriented = [], []
    for code in range(8):
        f_row = (lambda v: 7 - v) if code & 1 else (lambda v: v)
        f_col = (lambda v: 7 - v) if code & 2 else (lambda v: v)
        r2, c2 = f_row(r), f_col(c)
        source = c2 * 8 + r2 if code & 4 else r2 * 8 + c2
        oriented += [cell[:, None] == source[None, :]] * 2
        source = f_row(c) * 8 + f_col(r) if code & 4 else f_row(r) * 8 + f_col(c)
        unoriented += [cell[:, None] == source[None, :]] * 2
    spread = np.zeros((128, 1024), bool)
    spread[:64, :512] = pick.T
    spread[64:, 512:] = pick.T
    pick3 = np.zeros((1536, 192), bool)
    for k in range(3):
        pick3[k * 512 : (k + 1) * 512, k * 64 : (k + 1) * 64] = pick
    thrice = lambda m: np.concatenate([m] * 3, 0)
    asb = lambda m: jnp.asarray(m.astype(np.float32), BF16)
    return asb(pick3), asb(thrice(np.concatenate(oriented, 1))), asb(thrice(np.concatenate(unoriented, 1))), asb(thrice(spread))


def pieces(x):
    hi = x.astype(BF16)
    rest = x - hi.astype(F32)
    mid = rest.astype(BF16)
    low = (rest - mid.astype(F32)).astype(BF16)
    return hi, mid, low


def mm(a, b):
    return lax.dot_general(a, b, (((1,), (0,)), ((), ())), preferred_element_type=F32)


def beside(x):
    return jnp.concatenate(pieces(x), axis=1)


def folded(x, n):
    return (x[:, :n] + x[:, n : 2 * n]) + x[:, 2 * n :]


def pick_rows(onehot, x):
    return folded(mm(onehot, beside(x)), x.shape[1])


def iota(shape, axis):
    return lax.broadcasted_iota(jnp.int32, shape, axis)


def ones(mask):
    return jnp.where(mask, 1.0, 0.0).astype(BF16)


def column(row):
    n = row.shape[1]
    return jnp.sum(jnp.where(iota((n, n), 0) == iota((n, n), 1), row, 0.0), axis=1, keepdims=True)


def strip_mask():
    lane = iota((8, 512), 1)
    return (lane % 64) // 8 == iota((8, 512), 0)


def stack_field(ref_slice):
    return jnp.concatenate([ref_slice[:, i * 128 : (i + 1) * 128] for i in range(LAYERS)], axis=0)


def lookups(cells, fields, ks):
    n = cells.shape[0]
    whole = cells.astype(jnp.int32)
    row = ((whole & 4095) >> 7) * LAYERS + (whole >> 12)
    hot = ones(iota((n, 1024), 1) == row)
    here = iota((n, 128), 1) == (whole & 127)
    for k in ks:
        yield jnp.sum(jnp.where(here, folded(mm(hot, fields[k]), 128), 0.0), axis=1, keepdims=True)


def ranks(block, live):
    n = block.shape[1]
    alive = live[...] == 1
    target = block[...].astype(F32)
    key = jnp.where(alive, target, -1.0)
    key_col = column(key)
    same = key_col == key
    first, second = iota((n, n), 0), iota((n, n), 1)
    rank = jnp.sum(jnp.where(same & (first < second), 1.0, 0.0), axis=0, keepdims=True)
    rank_col = jnp.sum(jnp.where(same & (second < first), 1.0, 0.0), axis=1, keepdims=True)
    return jnp.where(alive, target * ROWS, -1.0), jnp.where(alive, target * ROWS + rank, -1.0), rank_col


def meta_rows(table, cell, rank_col):
    rows = table[...]
    lane = iota(rows.shape, 1)
    cell_col = column(cell[...].astype(F32))
    boil = jnp.maximum(rows, 0.0) + jnp.log1p(jnp.exp(-jnp.abs(rows)))
    sig = 1.0 / (1.0 + jnp.exp(-rows))
    kind = lane & 7
    meta = jnp.where(kind == 0, cell_col, jnp.where(kind == 1, boil[:, 1:2], jnp.where(kind == 2, sig[:, 2:3], jnp.where(kind == 3, 1.0, 0.0))))
    return jnp.where((lane >> 3).astype(F32) == rank_col, meta, 0.0)


def turned_tiles(faces, pick, oriented, unoriented, high_code, low_code):
    mask = strip_mask()
    strips = []
    for face in faces:
        for jt in range(8):
            strips.append(jnp.where(mask, face[:, jt * 512 : (jt + 1) * 512], 0.0))
    tiles = mm(beside(jnp.concatenate(strips, axis=0)), pick[...]).astype(BF16)
    turned = mm(tiles[:128], oriented[...])
    unturned = mm(tiles[128:], unoriented[...])

    def choose(x, code):
        out = x[:, :128]
        for o in range(1, 8):
            out = jnp.where(code == o, x[:, o * 128 : (o + 1) * 128], out)
        return out

    return [choose(turned[k * 64 : (k + 1) * 64], high_code) for k in range(2)] + [
        choose(unturned[k * 64 : (k + 1) * 64], low_code) for k in range(4)
    ]


def addressed(keys, values, out):
    keys, values = jnp.concatenate(keys, axis=1), jnp.concatenate(values, axis=0)
    out[...] = pick_rows(ones(iota((NB * ROWS, keys.shape[1]), 0).astype(F32) == keys), values)


def exchange_kernel(
    dif_in, species_in, flow_in, diffusion_in, lp_in, hp_in, lo_in, ho_in, table_in, block_in, cell_in, live_in,
    pick_in, oriented_in, unoriented_in, spread_in,
    z_sum, source, ghosts, parcels, change,
    dif, species, flow, edge, lp, hp, lo, ho, table, block, cell, live, pick, oriented, unoriented, spread,
    msg_a, msg_b, mid_a, mid_b, pack_a, recv_a, lists, forward, z_part, z_got, z_mine, fuel, fuel_col, fields, hot,
    load_sems, sems, recv_sems, near_send, near_recv, wide_send, wide_recv, local_sems, fuel_send, fuel_recv,
):
    b, q = lax.axis_index("blk"), lax.axis_index("sp")
    y, w = lax.div(b, NW), lax.rem(b, NW)
    pairs = (
        (species_in, species), (dif_in, dif), (flow_in.at[0, pl.ds(0, 8)], edge.at[0]), (diffusion_in.at[0, pl.ds(0, 8)], edge.at[1]),
        (table_in, table), (block_in, block), (live_in, live), (cell_in, cell), (lp_in, lp), (hp_in, hp), (lo_in, lo), (ho_in, ho),
        (pick_in, pick), (oriented_in, oriented), (unoriented_in, unoriented), (flow_in, flow), (spread_in, spread),
    )
    loads = [pltpu.make_async_copy(src, dst, load_sems.at[k]) for k, (src, dst) in enumerate(pairs)]
    for load in loads:
        load.start()
    barrier = pltpu.get_barrier_semaphore()

    for d in range(1, NQ):
        pl.semaphore_signal(barrier, inc=1, device_id=(b, lax.rem(q + d, NQ)), device_id_type=MESH)
    for d in range(1, NY):
        pl.semaphore_signal(barrier, inc=1, device_id=(lax.rem(y + d, NY) * NW + w, q), device_id_type=MESH)
    for d in range(1, NW):
        pl.semaphore_signal(barrier, inc=1, device_id=(y * NW + lax.rem(w + d, NW), q), device_id_type=MESH)
    loads[0].wait()
    loads[1].wait()

    d0, d1 = dif[0], dif[1]
    for k in range(NQ):
        z_part[k] = d0 * species[0, k * 8 : (k + 1) * 8] + d1 * species[1, k * 8 : (k + 1) * 8]
    for load in loads[2:15]:
        load.wait()
    to_block, to_slot, rank_col = ranks(block, live)
    up0, up1, lo0, lo1, fl, df = turned_tiles(
        [
            species[0, LAYERS - 1 : LAYERS, :], species[1, LAYERS - 1 : LAYERS, :], species[0, 0:1, :], species[1, 0:1, :],
            edge[0, 0:1, :], edge[1, 0:1, :],
        ],
        pick, oriented, unoriented, column(ho[...].astype(F32)), column(lo[...].astype(F32)),
    )
    left = iota((NB, 128), 1) < 64
    high, low = hp[...].astype(F32) * ROWS, lp[...].astype(F32) * ROWS
    by_block = iota((NB, 256), 0).astype(F32) * ROWS == to_block
    tile_keys = jnp.concatenate([high, low], axis=1)
    by_tile = ones(iota((NB, 2 * NB), 0).astype(F32) * ROWS == tile_keys)
    z_tiles = jnp.concatenate([jnp.where(left, d0 * up0 + d1 * up1, 0.0), jnp.where(left, 0.0, d0 * lo0 + d1 * lo1)], axis=0)
    edges = jnp.concatenate([jnp.zeros((NB, 128), F32), jnp.where(left, fl, df)], axis=0)
    picked = pick_rows(by_tile, jnp.concatenate([z_tiles, edges], axis=1))
    kinds = (pick_rows(ones(by_block), meta_rows(table, cell, rank_col)), picked[:, :128], picked[:, 128:])
    for k in range(KINDS):
        for to in range(NY):
            msg_a[to, k] = kinds[k][to * NW : (to + 1) * NW]
    pl.semaphore_wait(barrier, NQ + NY + NW - 3)

    def sp_copy(src, dst, k, d):
        return pltpu.make_async_remote_copy(
            src_ref=src, dst_ref=dst, send_sem=sems.at[k, d - 1], recv_sem=recv_sems.at[k, d - 1],
            device_id=(b, lax.rem(q + d, NQ)), device_id_type=MESH,
        )

    wide = JK // CHUNKS
    part = [pl.ds(c * wide, wide) for c in range(CHUNKS)]
    scatter = [
        [sp_copy(z_part.at[lax.rem(q + d, NQ), :, part[c]], z_got.at[d - 1, :, part[c]], c, d) for d in (2, 1, 3)]
        for c in range(CHUNKS)
    ]
    gather = [
        [sp_copy(z_mine.at[:, part[c]], z_sum.at[q, :, part[c]], CHUNKS + c, d) for d in (2, 1, 3)] for c in range(CHUNKS)
    ]

    def along_y(msg, mid, k):
        copies = []
        for d in (2, 1, 3):
            to = lax.rem(y + d, NY)
            copies.append(
                pltpu.make_async_remote_copy(
                    src_ref=msg.at[to], dst_ref=mid.at[y], send_sem=near_send.at[k, d - 1], recv_sem=near_recv.at[k, d - 1],
                    device_id=(to * NW + w, q), device_id_type=MESH,
                )
            )
        return copies

    def across(src, dst, k):
        def step(d, carry):
            to = lax.rem(w + 1 + lax.rem(d + 7, NW - 1), NW)
            pltpu.make_async_remote_copy(
                src_ref=src(to), dst_ref=dst(w), send_sem=wide_send.at[k], recv_sem=wide_recv.at[k],
                device_id=(y * NW + to, q), device_id_type=MESH,
            ).start()
            return carry

        lax.fori_loop(0, NW - 1, step, 0)

    most = pl.ds(0, NW - 1)
    first_a = along_y(msg_a, mid_a, 0)
    for copy in first_a:
        copy.start()
    for copies in scatter:
        for copy in copies:
            copy.start()

    loads[15].wait()
    loads[16].wait()

    def cut(i, carry):
        here = pl.ds(pl.multiple_of(i * 128, 128), 128)
        there = pl.ds(pl.multiple_of(i * LAYERS, LAYERS), LAYERS)
        fields[0, there, :] = beside(species[0, :, here])
        for k in range(3):
            fields[k + 1, there, :] = beside(flow[k, :, here])
        return carry

    mid_a[y] = msg_a[y]
    for copy in first_a:
        copy.wait_recv()
    packed = pack_a.reshape(NW * NW, 128)
    for src in range(NY):
        for k in range(KINDS):
            packed[pl.ds(src * KINDS + k, NW, stride=NW), :] = mid_a[src, k]
    rows_a = pl.ds(0, NY * KINDS)
    across(lambda to: pack_a.at[to, rows_a], lambda me: recv_a.at[me, rows_a], 0)
    recv_a[w] = pack_a[w]
    addressed(
        [to_slot, high + 6.0, low + 7.0],
        [table[...], jnp.where(left, up0, up1), jnp.where(left, lo0, lo1)],
        msg_b.reshape(NB * ROWS, 128),
    )
    keep_b = pltpu.make_async_copy(msg_b.at[y], mid_b.at[y], local_sems.at[0])
    first_b = along_y(msg_b, mid_b, 1)
    keep_b.start()
    for copy in first_b:
        copy.start()

    lax.fori_loop(0, CUT, cut, 0, unroll=2)
    lax.fori_loop(CUT, LAYERS, cut, 0, unroll=2)

    keep_b.wait()
    for copy in first_b:
        copy.wait_recv()
    across(lambda to: mid_b.at[:, to], lambda me: parcels.at[:, me], 1)
    keep_b = pltpu.make_async_copy(mid_b.at[:, w], parcels.at[:, w], local_sems.at[1])
    keep_b.start()

    def gather_part(c):
        for copy in scatter[c]:
            copy.wait_recv()
        total = (z_part[q, :, part[c]] + z_got[0, :, part[c]]) + (z_got[1, :, part[c]] + z_got[2, :, part[c]])
        z_mine[:, part[c]] = total
        for copy in gather[c]:
            copy.start()
        z_sum[q, :, part[c]] = total

    pltpu.make_async_copy(recv_a.at[most, rows_a], recv_a.at[most, rows_a], wide_recv.at[0]).wait()
    got = recv_a.reshape(NW * NW, 128)
    own, own_z, own_edges = (
        jnp.concatenate([got[pl.ds(src * KINDS + k, NW, stride=NW), :] for src in range(NY)], axis=0) for k in range(KINDS)
    )
    lists[q] = jnp.where(iota((NB // 2, 128), 1) < 64, own[: NB // 2], pltpu.roll(own[NB // 2 :], 64, 1))
    forward[q] = own_z
    onward = [sp_copy(lists.at[q], lists.at[q], 2 * CHUNKS, d) for d in (2, 1, 3)]
    onward_z = [sp_copy(forward.at[q], forward.at[q], 2 * CHUNKS + 1, d) for d in (2, 1, 3)]
    for copy in onward + onward_z:
        copy.start()

    got_b = parcels.reshape(NB * ROWS, 128)
    own_cells = jnp.concatenate([own[:, 8 * r : 8 * r + 1] for r in range(CAP)], axis=0)
    speeds = list(lookups(own_cells, fields, (1, 2, 3)))
    gather_part(0)

    @pl.when(q != 0)
    def _():
        for c in range(1, CHUNKS):
            gather_part(c)

    for copy in onward:
        copy.wait_recv()
    meta = []
    for k in range(NQ):
        both = lists[k]
        meta += [both, pltpu.roll(both, 64, 1)]
    meta = jnp.concatenate(meta, axis=0)
    shared = [
        pltpu.make_async_remote_copy(
            src_ref=fuel, dst_ref=fuel, send_sem=fuel_send.at[d - 1], recv_sem=fuel_recv, device_id=(b, d), device_id_type=MESH
        )
        for d in (2, 1, 3)
    ]

    @pl.when(q == 0)
    def _():
        lane = iota((NB * NQ, 128), 1)
        found = jnp.zeros((NB * NQ, 128), F32)
        cells = jnp.concatenate([meta[:, 8 * r : 8 * r + 1] for r in range(CAP)], axis=0)
        [value] = lookups(cells, fields, (0,))
        for r in range(CAP):
            found = jnp.where(lane == r, value[r * NB * NQ : (r + 1) * NB * NQ], found)
        fuel[...] = jnp.transpose(found)[:8]
        for copy in shared:
            copy.start()
        for c in range(1, CHUNKS):
            gather_part(c)

    meta_t = jnp.transpose(meta)
    cells = jnp.concatenate([meta_t[8 * r : 8 * r + 1, :] for r in range(CAP)], axis=1).astype(jnp.int32)
    row = ((cells & 4095) >> 7) * LAYERS + (cells >> 12)
    for m in range(4):
        hot[m * 256 : (m + 1) * 256, :] = ones(iota((256, NB * NQ * CAP), 0) + m * 256 == row)

    def fill_ghosts():
        keep_b.wait()
        pltpu.make_async_copy(parcels.at[:, most], parcels.at[:, most], wide_recv.at[1]).wait()
        low_sel = ones(iota((NB, NB), 1).astype(F32) == column(lp[...].astype(F32)))
        high_sel = ones(iota((NB, NB), 1).astype(F32) == column(hp[...].astype(F32)))
        for copy in onward_z:
            copy.wait_recv()
        z_tiles = (forward[0] + forward[1]) + (forward[2] + forward[3])
        below = pick_rows(low_sel, jnp.concatenate([got_b[pl.ds(6, NB, stride=ROWS), :], z_tiles], axis=1))
        above = pick_rows(
            high_sel, jnp.concatenate([got_b[pl.ds(7, NB, stride=ROWS), :], own_edges, z_tiles], axis=1)
        )
        tiles = jnp.concatenate([below[:, :128], above[:, :128], above[:, 128:256], jnp.where(left, below[:, 128:], above[:, 256:])], axis=0)
        spread_tiles = mm(beside(tiles), spread[...])
        mask = strip_mask()
        slots = ((0, 1), (3, 4), (6, 7), (2, 5))
        for g in range(4):
            for jt in range(8):
                strip = spread_tiles[g * 64 + jt * 8 : g * 64 + jt * 8 + 8]
                for side in range(2):
                    value = jnp.sum(jnp.where(mask, strip[:, side * 512 : (side + 1) * 512], 0.0), axis=0, keepdims=True)
                    ghosts[slots[g][side] : slots[g][side] + 1, jt * 512 : (jt + 1) * 512] = value

    fill_ghosts()

    @pl.when(q != 0)
    def _():
        shared[0].wait_recv()

    found_col = jnp.transpose(jnp.concatenate([fuel[...], jnp.zeros((120, NB * NQ), F32)], axis=0))
    fuel_col[...] = found_col
    lane = iota((NB * NQ, 128), 1)
    mass = []
    for r in range(CAP):
        k = 8 * r
        gone = meta[:, k + 1 : k + 2] * (meta[:, k + 2 : k + 3] - found_col[:, r : r + 1])
        at = meta[:, k : k + 1].astype(jnp.int32) & 127
        mass.append(beside(jnp.where(lane == at, gone, 0.0)))
    source[...] = folded(mm(hot[...], jnp.concatenate(mass, axis=0)), 128)

    own_fuel = fuel_col[pl.ds(pl.multiple_of(q * NB, NB), NB), :]
    lane = iota((NB, 128), 1)
    for r in range(CAP):
        k = 8 * r
        gone = own[:, k + 1 : k + 2] * (own[:, k + 2 : k + 3] - own_fuel[:, r : r + 1])
        drag = DRAG * own[:, k + 3 : k + 4]
        moved = jnp.where(lane == 0, -gone, 0.0)
        for c in range(3):
            moved = jnp.where(lane == 3 + c, drag * speeds[c][r * NB : (r + 1) * NB], moved)
        change[pl.ds(r, NB, stride=CAP), :] = moved

    @pl.when(q == 0)
    def _():
        for copy in shared:
            copy.wait_send()

    pltpu.make_async_copy(pack_a.at[most, rows_a], pack_a.at[most, rows_a], wide_send.at[0]).wait()
    pltpu.make_async_copy(mid_b.at[:, most], mid_b.at[:, most], wide_send.at[1]).wait()
    for copy in first_a + first_b:
        copy.wait_send()
    for copies in scatter:
        for copy in copies:
            copy.wait_send()
    for copy in onward + onward_z:
        copy.wait_send()
    for copies in gather:
        for copy in copies:
            copy.wait()


def final_kernel(
    dif, species, flow, diffusion, inv_volume, z_sum, source, ghosts, parcels, change, new_species, arrived, out, landed, out_sems,
):
    q = lax.axis_index("sp")
    d = (dif[0], dif[1])
    lane = iota((NB, 128), 1)
    keep = jnp.where((lane >= 3) & (lane <= 5), 1.0 - DRAG, 1.0)
    for r in range(CAP):
        landed[pl.ds(r, NB, stride=CAP), :] = parcels[pl.ds(r, NB, stride=ROWS), :] * keep + change[pl.ds(r, NB, stride=CAP), :]

    writes = [pltpu.make_async_copy(landed, arrived, out_sems.at[0])]
    writes[0].start()

    lane = iota((LAYERS, 128), 1)
    layer = iota((LAYERS, 128), 0)
    fuel = jnp.where(q == 0, 1.0, 0.0)
    right_half = lane >= 64
    inside = (lane & 63) != 0

    def strip(n, carry):
        i = LAYERS - 1 - n
        here = pl.ds(pl.multiple_of(i * 128, 128), 128)
        back = pl.ds(pl.multiple_of(jnp.maximum(i - 1, 0) * 128, 128), 128)
        beyond_wall = (i > 0) | right_half

        def below_of(x, ghost):
            return jnp.where(layer == 0, ghost, pltpu.roll(x, 1, 0))

        def before_of(x, previous):
            return pltpu.roll(jnp.where(right_half, previous, x), 64, 1)

        z = z_sum[:, here]
        g0, g1, g2 = diffusion[0, :, here], diffusion[1, :, here], diffusion[2, :, here]
        gt = ghosts[7:8, here]
        h0 = 0.5 * (flow[0, :, here] + g0 * (z - below_of(z, ghosts[2:3, here])))
        ht = 0.5 * (ghosts[6:7, here] + gt * (ghosts[5:6, here] - z[LAYERS - 1 :]))
        h1 = 0.5 * (flow[1, :, here] + g1 * (z - before_of(z, z_sum[:, back])))
        h2 = 0.5 * (flow[2, :, here] + g2 * (z - pltpu.roll(z, 1, 1)))
        h1, g1 = jnp.where(beyond_wall, h1, 0.0), jnp.where(beyond_wall, g1, 0.0)
        h2, g2 = jnp.where(inside, h2, 0.0), jnp.where(inside, g2, 0.0)
        half_inv = STEP * inv_volume[:, here]
        src = source[pl.ds(pl.multiple_of(i * LAYERS, LAYERS), LAYERS), :]
        onward = []
        for s in range(2):
            y = species[s, :, here]
            top = ghosts[3 + s : 4 + s, here]
            last = y[LAYERS - 1 :]
            y0 = below_of(y, ghosts[s : s + 1, here])
            y1 = before_of(y, species[s, :, back])
            y2 = pltpu.roll(y, 1, 1)
            f0 = h0 * (y + y0) - (g0 * d[s]) * (y - y0)
            ft = ht * (top + last) - (gt * d[s]) * (top - last)
            f1 = h1 * (y + y1) - (g1 * d[s]) * (y - y1)
            f2 = h2 * (y + y2) - (g2 * d[s]) * (y - y2)
            u0 = jnp.where(layer == LAYERS - 1, ft, pltpu.roll(f0, LAYERS - 1, 0))
            u1 = pltpu.roll(jnp.where(right_half, f1, carry[s]), 64, 1)
            u2 = pltpu.roll(f2, 127, 1)
            divergence = (u0 - f0) + ((u1 - f1) + (u2 - f2))
            delta = fuel if s == 0 else 0.0
            out[s, :, here] = y + half_inv * (src * (delta - y) - divergence)
            onward.append(f1)
        return tuple(onward)

    carry = (jnp.zeros((LAYERS, 128), F32),) * 2
    bounds = (0, 8, 16, 24, 28, 32)
    for g in range(5):
        carry = lax.fori_loop(bounds[g], bounds[g + 1], strip, carry, unroll=4)
        done = pl.ds((LAYERS - bounds[g + 1]) * 128, (bounds[g + 1] - bounds[g]) * 128)
        writes.append(pltpu.make_async_copy(out.at[:, :, done], new_species.at[:, :, done], out_sems.at[g + 1]))
        writes[-1].start()
    for write in writes:
        write.wait()


def spec(space=pltpu.VMEM):
    return pl.BlockSpec(memory_space=space)


HBM = pl.BlockSpec(memory_space=pltpu.HBM)


def params(**kw):
    return pltpu.CompilerParams(vmem_limit_bytes=VMEM_LIMIT, **kw)


def shape(*dims):
    return jax.ShapeDtypeStruct(dims, F32)


def body(
    species, interface_normal_flow, face_diffusion, inv_volume, diffusivity, low_partner, high_partner,
    low_orient, high_orient, droplet_table, parcel_block, parcel_cell, parcel_live,
):
    pick, oriented, unoriented, spread = constants()
    dma = pltpu.SemaphoreType.DMA
    vm = lambda *dims: pltpu.VMEM(dims, F32)
    iv = lambda *dims: pltpu.VMEM(dims, jnp.int32)
    bv = lambda *dims: pltpu.VMEM(dims, BF16)
    z_sum, source, ghosts, parcels, change = pl.pallas_call(
        exchange_kernel,
        out_shape=(shape(NQ, 8, JK), shape(1024, 128), shape(8, JK), shape(NY, NW, ROWS, 128), shape(NB * CAP, 128)),
        in_specs=[HBM] * 16,
        out_specs=(spec(),) * 5,
        scratch_shapes=[
            pltpu.SMEM((2,), F32), vm(2, LAYERS, JK), vm(3, LAYERS, JK), vm(2, 8, JK), *[iv(1, 64)] * 4, vm(256, 128), *[iv(1, 256)] * 3,
            bv(1536, 192), bv(192, 1024), bv(192, 1024), bv(384, 1024),
            vm(NY, KINDS, NW, 128), vm(NY, NW, ROWS, 128), vm(NY, KINDS, NW, 128), vm(NY, NW, ROWS, 128), *[vm(NW, NW, 128)] * 2,
            vm(NQ, NB // 2, 128), vm(NQ, NB, 128),
            vm(NQ, 8, JK), vm(3, 8, JK), vm(8, JK), vm(8, 256), vm(256, 128), bv(4, 1024, 384), bv(1024, 1536),
            dma((17,)), dma((2 * CHUNKS + 2, 3)), dma((2 * CHUNKS + 2, 3)), dma((2, 3)), dma((2, 3)), dma((2,)), dma((2,)), dma((2,)), dma((3,)), dma,
        ],
        compiler_params=params(collective_id=0, has_side_effects=True),
        name="exchange",
    )(*(pltpu.with_memory_space_constraint(x, pltpu.HBM) for x in (
        diffusivity, species, interface_normal_flow, face_diffusion, low_partner, high_partner, low_orient, high_orient,
        droplet_table, parcel_block.reshape(1, -1), parcel_cell.reshape(1, -1), parcel_live.reshape(1, -1),
        pick, oriented, unoriented, spread,
    )))
    new_species, arrived = pl.pallas_call(
        final_kernel,
        out_shape=(shape(2, LAYERS, JK), shape(384, 128)),
        in_specs=[pl.BlockSpec(memory_space=pltpu.SMEM)] + [spec()] * 9,
        out_specs=(HBM, HBM),
        scratch_shapes=[vm(2, LAYERS, JK), vm(NB * CAP, 128), dma((6,))],
        compiler_params=params(),
        name="final",
    )(
        diffusivity, species, interface_normal_flow, face_diffusion, inv_volume, z_sum.reshape(LAYERS, JK), source, ghosts,
        parcels.reshape(NB * ROWS, 128), change,
    )
    return new_species, arrived


def solution(mesh):
    placed = (
        P("sp", "blk", None), P(None, "blk", None), P(None, "blk", None), P("blk", None), P("sp"),
        P("blk", None), P("blk", None), P("blk", None), P("blk", None),
        P(("blk", "sp"), None), P(("blk", "sp"), None), P(("blk", "sp")), P(("blk", "sp")),
    )
    return jax.shard_map(
        body, mesh=mesh, in_specs=placed, out_specs=(P("sp", "blk", None), P(("blk", "sp"), None)), check_vma=False,
    )
```
